256 devices in a mesh: rows: 16 (over x, y), pts: 16 (over z, core).
Axes of the slice: x: 4, y: 4, z: 8, core: 2. Of those that a mesh axis runs over, the one named last changes fastest.
Arguments:
- env_desc: bfloat16 [8192, 1024], P('rows', 'pts'), may hold values from -6 to 6
- point_desc: bfloat16 [16384, 1024], P('pts', 'rows'), may hold values from -6 to 6
- pool_index: int32 [4096, 4], P('rows'), may hold values from 0 to 511
- pool_count: int32 [4096], P('rows'), may hold values from 1 to 4
- pool_weight: float32 [4096, 4], P('rows'), may hold values from -3 to 3
- row_dest: int32 [4096], P('rows'), may hold values from -1 to 2047, as said below
Outputs:
- design: float32 [2048, 16384], P('rows', 'pts')
- gram: float32 [16384, 16384], P('rows', 'pts')
The draws below stay inside these ranges and needn't reach their ends.
Inputs may be any that keep to these rules, and one draw needn't show every extreme that they name: Slot s pools environments (s // 256) * 512 + pool_index[s, j] of its own structure group. Slot s pools its first pool_count[s] entries. `row_dest`: -1 marks an empty slot; every row 0 .. 2047 is named by exactly one slot; the slots of one structure group (aligned blocks of 256 slots) name at most 16 rows of any aligned block of 128 rows, and in every draw some structure group names exactly 16 rows of every such block.
All inputs are finite; a program needn't handle non-finite values.
Results may differ from the reference program's by a relative error of at most 0.0003.
Values may be sent and summed in bfloat16 or wider, within the bound.
A program may use at most 128 MiB of HBM per device.

```python
import jax
import jax.numpy as jnp
from jax import lax

W = 1024
PTS = 16384
POOL = 4
E_DEV = 512
ROW_CAP = 256
R_BAL = 128
ENVS = 8192
SLOTS = 4096
ROWS = 2048
N_ROWS = 16
N_PTS = 16


def draw_row_dest(key, part):
    groups = N_ROWS
    subkeys = jax.random.split(jax.random.fold_in(key, 11), 4)
    half_count = groups // 2
    shifts = jax.random.randint(subkeys[0], (half_count,), -R_BAL, R_BAL + 1).astype(jnp.int32)
    shifts = shifts.at[0].set(R_BAL)
    changes = jnp.concatenate([shifts, -shifts])
    device_order = jax.random.permutation(subkeys[1], groups)
    live_counts = (R_BAL + changes)[device_order].astype(jnp.int32)
    first_rows = jnp.cumsum(live_counts) - live_counts
    slot_orders = jax.vmap(lambda subkey: jax.random.permutation(subkey, ROW_CAP))(jax.random.split(subkeys[2], groups))
    slot_rank = jnp.argsort(slot_orders, axis=1).astype(jnp.int32)
    live_slot = slot_rank < live_counts[:, None]
    global_row = first_rows[:, None] + slot_rank
    dest_group = global_row % groups
    within = jnp.clip(global_row // groups, 0, R_BAL - 1)
    positions = jax.vmap(lambda subkey: jax.random.permutation(subkey, R_BAL))(jax.random.split(subkeys[3], groups)).astype(jnp.int32)
    position = positions[dest_group, within]
    result = jnp.where(live_slot, dest_group * R_BAL + position, -1)
    return result.reshape(SLOTS).astype(jnp.int32)


def set_ends(drawn, own_key, low, largest):
    longest = drawn.shape.index(max(drawn.shape))
    spots = []
    for shift in (0, 1):
        where = [jax.random.randint(jax.random.fold_in(own_key, axis), (), 0, length) for axis, length in enumerate(drawn.shape)]
        where[longest] = (where[longest] + shift) % drawn.shape[longest]
        spots.append(tuple(where))
    return drawn.at[spots[0]].set(low).at[spots[1]].set(largest)


def steps_of(rng, extent, pieces, low, high):
    factor_of = 1.0
    for dim, parts in pieces:
        steps = jax.random.uniform(jax.random.fold_in(jax.random.fold_in(rng, 6), dim), (parts,), jnp.float32, low / len(pieces), high / len(pieces))
        factor_of = factor_of * jnp.repeat(jnp.exp(steps), extent[dim] // parts).reshape((-1,) + (1,) * (len(extent) - 1 - dim))
    return factor_of


def normal_values(stream_key, shape, scale, most, shards=(), held_as=jnp.bfloat16):
    gain = steps_of(stream_key, shape, shards, -0.22, 0.18) if shards else 1.0
    drawn = jax.random.normal(stream_key, shape, jnp.float32) * scale * gain
    return jnp.minimum(jnp.maximum(drawn, -most), most).astype(held_as)


def setup_inputs(seed: int = 0) -> dict:
    arg_keys = jax.random.split(jax.random.key(seed), 7)
    return {
        "env_desc": normal_values(arg_keys[0], (ENVS, W), 1.0, 6.0, ((0, 16), (1, 16))),
        "point_desc": normal_values(arg_keys[1], (PTS, W), 1.0, 6.0, ((0, 16), (1, 16))),
        "pool_index": set_ends(jax.random.randint(arg_keys[2], (SLOTS, POOL), 0, E_DEV), jax.random.fold_in(arg_keys[2], 1), 0, E_DEV - 1).astype(jnp.int32),
        "pool_count": set_ends(jax.random.randint(arg_keys[3], (SLOTS,), 1, POOL + 1), jax.random.fold_in(arg_keys[3], 1), 1, POOL).astype(jnp.int32),
        "pool_weight": normal_values(arg_keys[4], (SLOTS, POOL), 0.5, 3.0, ((0, 16),), jnp.float32),
        "row_dest": draw_row_dest(jax.random.fold_in(arg_keys[6], 71), 0),
    }


damping = 0.5


def kernel_values(left, right):
    products = lax.dot_general(left, right, (((1,), (1,)), ((), ())), preferred_element_type=jnp.float32)
    scaled = products * (left.shape[1] ** -0.5)
    squared = scaled * scaled
    return 0.25 * squared * squared


def live_weights(pool_count, pool_weight):
    members = jnp.arange(pool_weight.shape[1], dtype=jnp.int32)
    return jnp.where(members[None, :] < pool_count[:, None], pool_weight, 0.0)


def pool_rows(kernel_table, env_index, weights_live):
    pooled = jnp.zeros((env_index.shape[0], kernel_table.shape[1]), kernel_table.dtype)
    for member in range(env_index.shape[1]):
        pooled = pooled + weights_live[:, member:member + 1] * kernel_table[env_index[:, member]]
    return pooled


def reference(env_desc, point_desc, pool_index, pool_count, pool_weight, row_dest):
    group_start = (jnp.arange(SLOTS, dtype=jnp.int32) // ROW_CAP) * E_DEV
    env_index = pool_index + group_start[:, None]
    weights_live = live_weights(pool_count, pool_weight)
    point_blocks = point_desc.reshape(N_PTS, PTS // N_PTS, W)

    def one_block(points):
        return pool_rows(kernel_values(env_desc, points), env_index, weights_live)

    slot_rows = lax.map(one_block, point_blocks)
    slot_rows = jnp.transpose(slot_rows, (1, 0, 2)).reshape(SLOTS, PTS)
    target = jnp.where(row_dest >= 0, row_dest, ROWS)
    design = jnp.zeros((ROWS, PTS), jnp.float32).at[target].set(slot_rows, mode="drop")
    gram_full = lax.dot_general(design, design, (((0,), (0,)), ((), ())), precision=lax.Precision.HIGHEST, preferred_element_type=jnp.float32)
    gram_full = gram_full * (1.0 / ROWS)
    diagonal = jnp.arange(PTS, dtype=jnp.int32)
    gram_full = gram_full.at[diagonal, diagonal].add(damping)
    return design, gram_full
```

```python
import jax
import jax.numpy as jnp
from jax import lax
from jax.experimental import pallas as pl
from jax.experimental.pallas import tpu as pltpu
from jax.sharding import PartitionSpec as P

damping = 0.5
MESH = pl.DeviceIdType.MESH
f32, bf16, i16 = jnp.float32, jnp.bfloat16, jnp.int16
HALF = 528
CUT = 256
VMEM = pltpu.VMEM


def split_bf16(value):
    high = value.astype(bf16)
    return high, (value - high.astype(f32)).astype(bf16)


def where_am_i():
    r = lax.axis_index("rows")
    p = lax.axis_index("pts")
    return r // 4, r % 4, p // 2, p % 2


def plane_id(x, y, dx, dy):
    return ((x + dx + 4) % 4) * 4 + (y + dy + 4) % 4


def gather_keys():
    keys = []
    for half in (0, 1):
        for i in (0, 1, -1, 2):
            for j in (0, 1, -1, 2):
                if (i, j) == (0, 0):
                    continue
                two = j == 2 or (j == 0 and i == 2)
                keys += [(half, i, j, q) for q in ((0, 1) if two else (None,))]
    return {key: n for n, key in enumerate(keys)}


KEYS = gather_keys()


class TorusGather:
    def __init__(self, x, y, own, view, send_sems, recv_sems):
        self.x, self.y, self.own, self.view = x, y, own, view
        self.send_sems, self.recv_sems = send_sems, recv_sems
        self.sends = 0

    def offset(self, half, a, b):
        return (a, b) if half == 0 else (b, a)

    def block(self, half, i, j):
        return plane_id(self.x, self.y, *self.offset(half, i, j))

    def copy(self, half, i, j, q, to, key):
        target = plane_id(self.x, self.y, *self.offset(half, *to))
        block = self.block(half, i, j)
        src = self.own(half, q) if (i, j) == (0, 0) else self.view(block, half, q)
        pltpu.make_async_remote_copy(
            src_ref=src,
            dst_ref=self.view(block, half, q),
            send_sem=self.send_sems.at[self.sends],
            recv_sem=self.recv_sems.at[KEYS[key]],
            device_id={"rows": target},
            device_id_type=MESH,
        ).start()
        self.sends += 1

    def wait(self, half, i, j, q):
        ref = self.view(self.block(half, i, j), half, q)
        pltpu.make_async_copy(ref, ref, self.recv_sems.at[KEYS[(half, i, j, q)]]).wait()

    def start(self):
        for half in (0, 1):
            for d in (1, -1):
                self.copy(half, 0, 0, None, (d, 0), (half, -d, 0, None))
        for half in (0, 1):
            for d in (1, -1):
                self.copy(half, 0, 0, None, (0, d), (half, 0, -d, None))

    def first(self):
        for half in (0, 1):
            for d in (1, -1):
                q = 0 if d == 1 else 1
                self.wait(half, -d, 0, None)
                self.copy(half, -d, 0, q, (d, 0), (half, 2, 0, q))
                for e in (1, -1):
                    self.copy(half, -d, 0, None, (0, e), (half, -d, -e, None))

    def across(self, i):
        for half in (0, 1):
            for d in (1, -1):
                q = 0 if d == 1 else 1
                self.wait(half, i, -d, None)
                self.copy(half, i, -d, q, (0, d), (half, i, 2, q))

    def far(self):
        for half in (0, 1):
            for q in (0, 1):
                self.wait(half, 2, 0, q)
            for e in (1, -1):
                self.copy(half, 2, 0, None, (0, e), (half, 2, -e, None))

    def last(self, i):
        for half in (0, 1):
            for q in (0, 1):
                self.wait(half, i, 2, q)

    def drain(self):
        n = 0
        for whole in self.order():
            ref = self.own(0, whole)
            pltpu.make_async_copy(ref, ref, self.send_sems.at[n]).wait()
            n += 1

    def order(self):
        sizes = [None] * 8
        for half in (0, 1):
            for d in (1, -1):
                sizes += [0 if d == 1 else 1, None, None]
        sizes += [0, 1] * 2
        sizes += [None] * 4
        sizes += [0, 1] * 2
        sizes += [0, 1] * 2
        sizes += [0, 1] * 2
        return sizes


ORDER = [(0, 0), (1, 0), (-1, 0), (0, 1), (0, -1), (1, 1), (1, -1), (-1, 1), (-1, -1),
         (0, 2), (2, 0), (1, 2), (-1, 2), (2, 1), (2, -1), (2, 2)]
LAG = 2
PAIRS = 8
READY = 6


def block_of(x, y, n):
    dx = jnp.int32(0)
    dy = jnp.int32(0)
    for k, (a, b) in enumerate(ORDER):
        hit = (n == k).astype(jnp.int32)
        dx = dx + hit * (a + 4)
        dy = dy + hit * (b + 4)
    return ((x + dx) % 4) * 4 + (y + dy) % 4


def column_scale(tile, factor):
    parts = tile.astype(jnp.int32).astype(f32)
    return jnp.exp2(parts[:8]) * (parts[8:] * (factor / 32767.0))


def as_i16(value):
    return jnp.clip(jnp.round(value), -32767.0, 32767.0).astype(jnp.int32).astype(i16)


def gram_kernel(enc_ref, out_ref, buf, hp, lp, hrt, lrt, sends, recvs, zsends, zrecvs, own_sem):
    x, y, z, c = where_am_i()
    r = x * 4 + y
    z0, c0 = r // 2, r % 2
    dz = (z - z0 + 8) % 8
    root_chip = dz == 0
    root = jnp.logical_and(root_chip, c == c0)
    up = {"pts": ((z + 1) % 8) * 2}
    down = {"pts": ((z + 7) % 8) * 2 + 1}
    other = {"pts": z * 2 + 1 - c}
    barrier = pltpu.get_barrier_semaphore()
    for dx, dy in ((1, 0), (-1, 0), (0, 1), (0, -1)):
        pl.semaphore_signal(barrier, inc=1, device_id={"rows": plane_id(x, y, dx, dy)}, device_id_type=MESH)
    for dc in (0, 1):
        for target in ((z + 1) % 8, (z + 7) % 8):
            pl.semaphore_signal(barrier, inc=1, device_id={"pts": target * 2 + dc}, device_id_type=MESH)
    pl.semaphore_signal(barrier, inc=1, device_id=other, device_id_type=MESH)
    pl.semaphore_wait(barrier, 9)

    def cut(ref, q):
        if q is None:
            return ref
        return ref.at[pl.ds(0, CUT)] if q == 0 else ref.at[pl.ds(CUT, HALF - CUT)]

    gather = TorusGather(
        x, y,
        lambda half, q: cut(enc_ref.at[half], q),
        lambda block, half, q: cut(buf.at[0, block, half], q),
        sends, recvs,
    )
    gather.start()
    own_copy = pltpu.make_async_copy(enc_ref, buf.at[0, r], own_sem)
    own_copy.start()

    rows = r * 1024 + lax.broadcasted_iota(jnp.int32, (128, 1024), 0)
    cols = (z * 2 + c) * 1024 + lax.broadcasted_iota(jnp.int32, (128, 1024), 1)

    @pl.loop(0, 8)
    def _(m):
        out_ref[pl.ds(pl.multiple_of(m * 128, 128), 128), :] = jnp.where(rows + m * 128 == cols, damping, 0.0).astype(f32)

    own_copy.wait()
    gather.first()
    gather.across(0)
    gather.far()
    gather.across(1)
    gather.across(-1)
    gather.across(2)
    for i in (0, 1, -1, 2):
        gather.last(i)

    def z_copy(block, half, target, n, k):
        return pltpu.make_async_remote_copy(
            src_ref=buf.at[jnp.where(root, 0, 1), block, half],
            dst_ref=buf.at[1, block, half],
            send_sem=zsends.at[n, k],
            recv_sem=zrecvs.at[n, half],
            device_id=target,
            device_id_type=MESH,
        )

    def z_wait(block, half, n):
        ref = buf.at[1, block, half]
        pltpu.make_async_copy(ref, ref, zrecvs.at[n, half]).wait()

    hops = jnp.where(c == 0, dz, (8 - dz) % 8)
    not_end = jnp.where(c == 0, dz != 7, dz != 1)

    def pass_on(n):
        block = block_of(x, y, n)

        @pl.when(root)
        def _():
            z_copy(block, 0, up, n, 0).start()
            z_copy(block, 1, down, n, 1).start()
            z_copy(block, 0, other, n, 2).start()
            z_copy(block, 1, other, n, 3).start()

        for half in (0, 1):
            @pl.when(jnp.logical_and(jnp.logical_not(root_chip), c == half))
            def _():
                z_wait(block, half, n)

                @pl.when(not_end)
                def _():
                    z_copy(block, half, up if half == 0 else down, n, 0).start()

                z_copy(block, half, other, n, 1).start()

    def drained(n):
        ref = buf.at[0, 0, 0]

        @pl.when(root)
        def _():
            for k in range(4):
                pltpu.make_async_copy(ref, ref, zsends.at[n, k]).wait()

        @pl.when(jnp.logical_not(root_chip))
        def _():
            @pl.when(not_end)
            def _():
                pltpu.make_async_copy(ref, ref, zsends.at[n, 0]).wait()

            pltpu.make_async_copy(ref, ref, zsends.at[n, 1]).wait()

    from_root = jnp.where(root, 0, 1)

    def decode(n, place):
        block = block_of(x, y, n)
        for half in (0, 1):
            @pl.when(jnp.logical_and(jnp.logical_not(root), jnp.logical_or(root_chip, c != half)))
            def _():
                z_wait(block, half, n)

        scale_p = column_scale(buf[0, block, 0, pl.ds(512, 16), :], 2.0 ** -11)
        scale_r = column_scale(buf[from_root, block, 0, pl.ds(512, 16), :], 1.0)
        for j in range(8):
            cols = slice(128 * j, 128 * j + 128)
            for half in (0, 1):
                part = buf[0, block, half, pl.ds(64 * j, 64), :].astype(jnp.int32).astype(f32) * scale_p[j : j + 1, :]
                high, low = split_bf16(part)
                spot = pl.ds(place * 128 + half * 64, 64)
                hp[spot, cols] = high
                lp[spot, cols] = low
            both = jnp.concatenate(
                [buf[from_root, block, half, pl.ds(64 * j, 64), :].astype(jnp.int32).astype(f32) for half in (0, 1)], axis=0
            )
            high, low = split_bf16((both * scale_r[j : j + 1, :]).T)
            hrt[cols, pl.ds(place * 128, 128)] = high
            lrt[cols, pl.ds(place * 128, 128)] = low

    def multiply():
        right = jnp.concatenate([hp[...], lp[...], hp[...]], axis=0)

        @pl.loop(0, 4)
        def _(m):
            spot = pl.ds(pl.multiple_of(m * 256, 256), 256)
            high = hrt[spot, :]
            left = jnp.concatenate([high, high, lrt[spot, :]], axis=1)
            out_ref[spot, :] += jnp.dot(left, right, preferred_element_type=f32)

    far_hops = jnp.maximum(hops, (8 - hops) % 8)

    @pl.loop(0, 16 + 8 * LAG + 2)
    def _(s):
        n = s - hops * LAG

        @pl.when(jnp.logical_and(n >= 0, n < 16))
        def _():
            pass_on(n)

        m = s - far_hops * LAG - 1

        @pl.when(jnp.logical_and(jnp.logical_and(m >= 0, m < 16), m % 2 == 1))
        def _():
            decode(m - 1, 0)
            decode(m, 1)
            multiply()

    gather.drain()

    @pl.loop(0, 16)
    def _(n):
        drained(n)


def gram_of(enc):
    return pl.pallas_call(
        gram_kernel,
        out_shape=jax.ShapeDtypeStruct((1024, 1024), f32),
        in_specs=[pl.BlockSpec(memory_space=VMEM)],
        out_specs=pl.BlockSpec(memory_space=VMEM),
        scratch_shapes=[
            VMEM((2, 16, 2, HALF, 128), i16),
            VMEM((256, 1024), bf16),
            VMEM((256, 1024), bf16),
            VMEM((1024, 256), bf16),
            VMEM((1024, 256), bf16),
            pltpu.SemaphoreType.DMA((40,)),
            pltpu.SemaphoreType.DMA((40,)),
            pltpu.SemaphoreType.DMA((16, 4)),
            pltpu.SemaphoreType.DMA((16, 2)),
            pltpu.SemaphoreType.DMA(()),
        ],
        compiler_params=pltpu.CompilerParams(collective_id=1, has_side_effects=True, vmem_limit_bytes=56 << 20),
        name="gram",
    )(enc)


def design_kernel(feat_ref, meta_ref, points_ref, design_ref, enc_ref, lhs):
    lane = lax.broadcasted_iota(jnp.int32, (128, 128), 1)
    for k in range(8):
        for pair in (0, 1):
            a = feat_ref[2 * k, pair].astype(f32)
            b = feat_ref[2 * k + 1, pair].astype(f32)
            even = jnp.where(lane < 64, a, pltpu.roll(b, 64, 1))
            odd = jnp.where(lane < 64, pltpu.roll(a, 64, 1), b)
            lhs[pl.ds(pair * 256, 128), pl.ds(k * 128, 128)] = even.astype(bf16)
            lhs[pl.ds(pair * 256 + 128, 128), pl.ds(k * 128, 128)] = odd.astype(bf16)
    meta = meta_ref[...]
    weights = [meta[:, j : j + 1] + meta[:, j + 4 : j + 5] + meta[:, j + 8 : j + 9] for j in range(4)]
    tops, bottoms = [], []
    for t in range(4):
        cols = pl.ds(t * 256, 256)
        products = jnp.dot(lhs[...], points_ref[:, cols], preferred_element_type=f32)
        scaled = products * (1.0 / 32.0)
        squared = scaled * scaled
        values = 0.25 * squared * squared
        rows = jnp.zeros((128, 256), f32)
        for j in range(4):
            rows = rows + weights[j] * values[j * 128 : (j + 1) * 128]
        design_ref[:, cols] = rows
        largest = jnp.maximum(jnp.max(jnp.abs(rows), axis=0, keepdims=True), 1e-30)
        exponent = jnp.floor(jnp.log2(largest)) - 14.0
        mantissa = jnp.minimum(jnp.ceil(largest * jnp.exp2(-exponent)), 32767.0)
        coded = rows * (32767.0 / (mantissa * jnp.exp2(exponent)))
        for u in range(2):
            j = 2 * t + u
            part = coded[:, 128 * u : 128 * u + 128]
            enc_ref[0, pl.ds(64 * j, 64), :] = as_i16(part[:64])
            enc_ref[1, pl.ds(64 * j, 64), :] = as_i16(part[64:])
            tops.append(exponent[:, 128 * u : 128 * u + 128])
            bottoms.append(mantissa[:, 128 * u : 128 * u + 128])
    tile = as_i16(jnp.concatenate(tops + bottoms, axis=0))
    enc_ref[0, pl.ds(512, 16), :] = tile
    enc_ref[1, pl.ds(512, 16), :] = tile


def design_of(feat, meta, points):
    return pl.pallas_call(
        design_kernel,
        out_shape=(jax.ShapeDtypeStruct((128, 1024), f32), jax.ShapeDtypeStruct((2, HALF, 128), i16)),
        in_specs=[pl.BlockSpec(memory_space=VMEM)] * 3,
        out_specs=(pl.BlockSpec(memory_space=VMEM), pl.BlockSpec(memory_space=VMEM)),
        scratch_shapes=[VMEM((512, 1024), bf16)],
        name="design",
    )(feat, meta, points)


def outbox_of(env, pool_index, pool_count, pool_weight, row_dest):
    members = jnp.arange(4, dtype=jnp.int32)
    live = row_dest >= 0
    dest = jnp.where(live, row_dest // 128, 16)
    within = jnp.where(live, row_dest % 128 + 1, 0)
    owner = (dest[:, None] == jnp.arange(16, dtype=jnp.int32)[None, :]).astype(f32)
    ids = jnp.arange(256, dtype=jnp.int32)
    earlier = jnp.dot((ids[:, None] > ids[None, :]).astype(f32), owner)
    rank = jnp.sum(earlier * owner, axis=1).astype(jnp.int32)
    place = jnp.where(live, dest * 16 + rank, 256)
    move = (ids[:, None] == place[None, :]).astype(bf16)
    envs = jnp.arange(512, dtype=jnp.int32)
    picked = [
        jnp.dot((pool_index[:, j : j + 1] == envs[None, :]).astype(bf16), env, preferred_element_type=f32).astype(bf16)
        for j in range(4)
    ]
    weight = jnp.where(members[None, :] < pool_count[:, None], pool_weight, 0.0)
    high = lax.reduce_precision(weight, 8, 7)
    mid = lax.reduce_precision(weight - high, 8, 7)
    low = weight - high - mid
    meta = jnp.concatenate([high, mid, low, within[:, None].astype(f32), jnp.zeros((256, 115), f32)], axis=1).astype(bf16)
    everything = jnp.concatenate(picked + [meta], axis=1)
    moved = jnp.dot(move, everything, preferred_element_type=f32).astype(bf16)
    return jnp.concatenate([moved[:, 128 * k : 128 * k + 128].reshape(16, 16, 128) for k in range(3)], axis=1)


def on_device(env_desc, point_desc, pool_index, pool_count, pool_weight, row_dest):
    points = lax.all_gather(point_desc.T, "rows", axis=0, tiled=True)
    outbox = outbox_of(env_desc, pool_index, pool_count, pool_weight, row_dest)
    inbox = lax.all_to_all(outbox, "rows", split_axis=0, concat_axis=0, tiled=True)
    parts = [inbox[:, 16 * k : 16 * k + 16].reshape(256, 128) for k in range(3)]
    spots = parts[2][:, 12:13].astype(f32)
    put = (spots == jnp.arange(1, 129, dtype=f32)[None, :]).astype(bf16)
    placed = [lax.dot_general(put, part, (((0,), (0,)), ((), ())), preferred_element_type=f32) for part in parts]
    mine = jnp.stack([placed[0].astype(bf16), placed[1].astype(bf16)])
    feat = lax.all_gather(mine, "pts", axis=0)
    design, enc = design_of(feat, placed[2], points)
    return design, gram_of(enc)


def solution(mesh):
    in_specs = (
        P("rows", "pts"),
        P("pts", "rows"),
        P("rows", None),
        P("rows"),
        P("rows", None),
        P("rows"),
    )
    out_specs = (P("rows", "pts"), P("rows", "pts"))
    return jax.shard_map(
        on_device, mesh=mesh, in_specs=in_specs, out_specs=out_specs, check_vma=False
    )
```

```python
import jax
import jax.numpy as jnp
from jax import lax
from jax.experimental import pallas as pl
from jax.experimental.pallas import tpu as pltpu
from jax.sharding import PartitionSpec as P

damping = 0.5
MESH = pl.DeviceIdType.MESH
f32, bf16, i16 = jnp.float32, jnp.bfloat16, jnp.int16
HALF = 528
CUT = 256
VMEM = pltpu.VMEM


def split_bf16(value):
    high = value.astype(bf16)
    return high, (value - high.astype(f32)).astype(bf16)


def where_am_i():
    r = lax.axis_index("rows")
    p = lax.axis_index("pts")
    return r // 4, r % 4, p // 2, p % 2


def plane_id(x, y, dx, dy):
    return ((x + dx + 4) % 4) * 4 + (y + dy + 4) % 4


def gather_keys():
    keys = []
    for half in (0, 1):
        for i in (0, 1, -1, 2):
            for j in (0, 1, -1, 2):
                if (i, j) == (0, 0):
                    continue
                two = j == 2 or (j == 0 and i == 2)
                keys += [(half, i, j, q) for q in ((0, 1) if two else (None,))]
    return {key: n for n, key in enumerate(keys)}


KEYS = gather_keys()


class TorusGather:
    def __init__(self, x, y, view, send_sems, recv_sems):
        self.x, self.y, self.view = x, y, view
        self.send_sems, self.recv_sems = send_sems, recv_sems
        self.sends = 0

    def offset(self, half, a, b):
        return (a, b) if half == 0 else (b, a)

    def block(self, half, i, j):
        return plane_id(self.x, self.y, *self.offset(half, i, j))

    def copy(self, half, i, j, q, to, key):
        target = plane_id(self.x, self.y, *self.offset(half, *to))
        block = self.block(half, i, j)
        pltpu.make_async_remote_copy(
            src_ref=self.view(block, half, q),
            dst_ref=self.view(block, half, q),
            send_sem=self.send_sems.at[self.sends],
            recv_sem=self.recv_sems.at[KEYS[key]],
            device_id={"rows": target},
            device_id_type=MESH,
        ).start()
        self.sends += 1

    def wait(self, half, i, j, q):
        ref = self.view(self.block(half, i, j), half, q)
        pltpu.make_async_copy(ref, ref, self.recv_sems.at[KEYS[(half, i, j, q)]]).wait()

    def start(self):
        for half in (0, 1):
            for d in (1, -1):
                self.copy(half, 0, 0, None, (d, 0), (half, -d, 0, None))
        for half in (0, 1):
            for d in (1, -1):
                self.copy(half, 0, 0, None, (0, d), (half, 0, -d, None))

    def first(self):
        for half in (0, 1):
            for d in (1, -1):
                q = 0 if d == 1 else 1
                self.wait(half, -d, 0, None)
                self.copy(half, -d, 0, q, (d, 0), (half, 2, 0, q))
                for e in (1, -1):
                    self.copy(half, -d, 0, None, (0, e), (half, -d, -e, None))

    def across(self, i):
        for half in (0, 1):
            for d in (1, -1):
                q = 0 if d == 1 else 1
                self.wait(half, i, -d, None)
                self.copy(half, i, -d, q, (0, d), (half, i, 2, q))

    def far(self):
        for half in (0, 1):
            for q in (0, 1):
                self.wait(half, 2, 0, q)
            for e in (1, -1):
                self.copy(half, 2, 0, None, (0, e), (half, 2, -e, None))

    def last(self, i):
        for half in (0, 1):
            for q in (0, 1):
                self.wait(half, i, 2, q)

    def drain(self):
        n = 0
        for whole in self.order():
            ref = self.view(0, 0, whole)
            pltpu.make_async_copy(ref, ref, self.send_sems.at[n]).wait()
            n += 1

    def order(self):
        sizes = [None] * 8
        for half in (0, 1):
            for d in (1, -1):
                sizes += [0 if d == 1 else 1, None, None]
        sizes += [0, 1] * 2
        sizes += [None] * 4
        sizes += [0, 1] * 2
        sizes += [0, 1] * 2
        sizes += [0, 1] * 2
        return sizes


ORDER = [(0, 0), (1, 0), (-1, 0), (0, 1), (0, -1), (2, 0), (1, 1), (1, -1), (-1, 1), (-1, -1),
         (0, 2), (2, 1), (2, -1), (1, 2), (-1, 2), (2, 2)]
FIRST_SLOT = 2
SLOTS = 50


def signed(value):
    return value - (1 << 32) if value >= 1 << 31 else value


FIRST_STEPS = signed(sum((a % 4) << (2 * n) for n, (a, b) in enumerate(ORDER)))
SECOND_STEPS = signed(sum((b % 4) << (2 * n) for n, (a, b) in enumerate(ORDER)))
PLANE = [(dx, dy) for dx in range(4) for dy in range(4) if (dx, dy) != (0, 0)]


def block_of(x, y, half, n):
    a = (jnp.int32(FIRST_STEPS) >> (2 * n)) & 3
    b = (jnp.int32(SECOND_STEPS) >> (2 * n)) & 3
    dx = jnp.where(half == 0, a, b)
    dy = jnp.where(half == 0, b, a)
    return ((x + dx) % 4) * 4 + (y + dy) % 4


def hop_slots(hops):
    return (7 * hops + 3) // 4


def column_scale(tile, factor):
    parts = tile.astype(jnp.int32).astype(f32)
    return jnp.exp2(parts[:8]) * (parts[8:] * (factor / 32767.0))


def as_i16(value):
    return jnp.clip(jnp.round(value), -32767.0, 32767.0).astype(jnp.int32).astype(i16)


def iota(shape, axis):
    return lax.broadcasted_iota(jnp.int32, shape, axis)


def one_hot(test):
    return jnp.where(test, 1.0, 0.0).astype(bf16)


def dot(a, b, ca=1, cb=0):
    return lax.dot_general(a, b, (((ca,), (cb,)), ((), ())), preferred_element_type=f32)


def fill_outbox(env_ref, index_ref, count_ref, weight_ref, dest_ref, outbox):
    row = dest_ref[...]
    live = row >= 0
    dest = row >> 7
    owner = jnp.where(dest == iota((256, 128), 1), 1.0, 0.0)
    earlier = dot(one_hot(iota((256, 256), 0) > iota((256, 256), 1)), owner.astype(bf16))
    rank = jnp.sum(earlier * owner, axis=1, keepdims=True)
    place = jnp.where(live, dest.astype(f32) * 16.0 + rank, 999.0)
    move = one_hot(place == iota((256, 256), 1).astype(f32))
    env = env_ref[...]
    sides = [dot(env, one_hot(iota((64, 128), 0) + 64 * k == iota((64, 128), 1))).astype(bf16) for k in (0, 1)]
    index = index_ref[...]
    envs = iota((256, 512), 1)
    picked = [
        (dot(one_hot(index[:, 2 * k : 2 * k + 1] == envs), sides[0])
         + dot(one_hot(index[:, 2 * k + 1 : 2 * k + 2] == envs), sides[1])).astype(bf16)
        for k in (0, 1)
    ]
    weight = jnp.where(iota((256, 4), 1) < count_ref[...], weight_ref[...], 0.0)
    lane = iota((256, 128), 1)
    within = jnp.where(live, (row & 127) + 1, 0).astype(f32)
    meta = jnp.where(lane == 12, within, 0.0)
    rest = weight
    for k in range(3):
        part = rest.astype(bf16).astype(f32)
        rest = rest - part
        for j in range(4):
            meta = jnp.where(lane == 4 * k + j, part[:, j : j + 1], meta)
    moved = dot(move, jnp.concatenate(picked + [meta.astype(bf16)], axis=1), 0, 0).astype(bf16)
    for d in range(16):
        for k in range(3):
            outbox[d, 16 * k : 16 * k + 16, :] = moved[16 * d : 16 * d + 16, 128 * k : 128 * k + 128]


def whole_kernel(env_ref, desc_ref, index_ref, count_ref, weight_ref, dest_ref, design_ref, out_ref,
                 points, outbox, inbox, feats, meta, lhs, buf, hp, lp, hrt, lrt,
                 psend, precv, osend, orecv, own_sem, fsend, frecv, frecv2, sends, recvs, zsends, zrecvs):
    x, y, z, c = where_am_i()
    r = x * 4 + y
    p = z * 2 + c
    z0, c0 = r // 2, r % 2
    dz = (z - z0 + 8) % 8
    root_chip = dz == 0
    root = jnp.logical_and(root_chip, c == c0)
    up = {"pts": ((z + 1) % 8) * 2}
    down = {"pts": ((z + 7) % 8) * 2 + 1}
    other = {"pts": z * 2 + 1 - c}
    along = {1: {"pts": ((z + 1) % 8) * 2 + c}, -1: {"pts": ((z + 7) % 8) * 2 + c}}
    barrier = pltpu.get_barrier_semaphore()
    for dx, dy in PLANE:
        pl.semaphore_signal(barrier, inc=1, device_id={"rows": plane_id(x, y, dx, dy)}, device_id_type=MESH)
    for dc in (0, 1):
        for target in ((z + 1) % 8, (z + 7) % 8):
            pl.semaphore_signal(barrier, inc=1, device_id={"pts": target * 2 + dc}, device_id_type=MESH)
    pl.semaphore_signal(barrier, inc=1, device_id=other, device_id_type=MESH)

    own = dot(one_hot(iota((64, 64), 0) == iota((64, 64), 1)), desc_ref[...], 1, 1).astype(bf16)
    points[r, 0] = own[:32]
    points[r, 1] = own[32:]
    fill_outbox(env_ref, index_ref, count_ref, weight_ref, dest_ref, outbox)
    pl.semaphore_wait(barrier, 20)

    def post(k, dx, dy):
        target = plane_id(x, y, dx, dy)
        return pltpu.make_async_remote_copy(
            src_ref=outbox.at[target], dst_ref=inbox.at[r], send_sem=osend.at[k], recv_sem=orecv.at[k],
            device_id={"rows": target}, device_id_type=MESH,
        )

    for k, (dx, dy) in enumerate(PLANE):
        post(k, dx, dy).start()
    own_copy = pltpu.make_async_copy(outbox.at[r], inbox.at[r], own_sem)
    own_copy.start()

    def points_view(block, half, q):
        return points.at[block, half] if q is None else points.at[block, half, pl.ds(16 * q, 16)]

    spread = TorusGather(x, y, points_view, psend, precv)
    spread.start()

    rows = r * 1024 + iota((128, 1024), 0)
    cols = p * 1024 + iota((128, 1024), 1)

    @pl.loop(0, 8)
    def _(m):
        out_ref[pl.ds(pl.multiple_of(m * 128, 128), 128), :] = jnp.where(rows + m * 128 == cols, damping, 0.0)

    spread.first()
    own_copy.wait()
    for k, (dx, dy) in enumerate(PLANE):
        ref = inbox.at[plane_id(x, y, -dx, -dy)]
        pltpu.make_async_copy(ref, ref, orecv.at[k]).wait()
    arrived = [jnp.concatenate([inbox[g, 16 * k : 16 * k + 16, :] for g in range(16)], axis=0) for k in range(3)]
    spots = arrived[2][:, 12:13].astype(f32)
    put = one_hot(spots == (iota((256, 128), 1) + 1).astype(f32))
    placed = dot(put, jnp.concatenate(arrived, axis=1), 0, 0)
    feats[p, 0] = placed[:, :128].astype(bf16)
    feats[p, 1] = placed[:, 128:256].astype(bf16)
    meta[...] = placed[:, 256:]

    def feat_copy(offset, pair, target, n, recv):
        ref = feats.at[((z + offset + 8) % 8) * 2 + c]
        if pair is not None:
            ref = ref.at[pair]
        return pltpu.make_async_remote_copy(
            src_ref=ref, dst_ref=ref, send_sem=fsend.at[n], recv_sem=recv, device_id=target, device_id_type=MESH
        )

    def feat_wait(owner, sem, pair=None):
        ref = feats.at[owner]
        if pair is not None:
            ref = ref.at[pair]
        pltpu.make_async_copy(ref, ref, sem).wait()

    feat_copy(0, None, along[1], 0, frecv.at[0]).start()
    feat_copy(0, None, along[-1], 1, frecv.at[4]).start()
    feat_copy(0, None, other, 2, frecv2.at[0]).start()

    def feat_step(k):
        for d, base in ((1, 0), (-1, 4)):
            pair = (0 if d == 1 else 1) if k == 3 else None
            n = 3 + 4 * (k - 1) + (0 if d == 1 else 2)
            feat_wait(((z - d * k + 8) % 8) * 2 + c, frecv.at[base + k - 1])
            feat_copy(-d * k, pair, along[d], n, frecv.at[base + k]).start()
            feat_copy(-d * k, None, other, n + 1, frecv2.at[(8 - d * k) % 8]).start()

    spread.across(0)
    feat_step(1)
    spread.far()
    feat_step(2)
    spread.across(1)
    feat_step(3)
    spread.across(-1)
    for d, base, pair in ((1, 0, 0), (-1, 4, 1)):
        feat_wait(((z + 4) % 8) * 2 + c, frecv.at[base + 3], pair)
    feat_copy(4, None, other, 15, frecv2.at[4]).start()
    for k in range(8):
        feat_wait(((z + k) % 8) * 2 + 1 - c, frecv2.at[k])
    spread.across(2)
    lane = iota((128, 128), 1)
    for k in range(8):
        for pair in (0, 1):
            a = feats[2 * k, pair].astype(f32)
            b = feats[2 * k + 1, pair].astype(f32)
            even = jnp.where(lane < 64, a, pltpu.roll(b, 64, 1))
            odd = jnp.where(lane < 64, pltpu.roll(a, 64, 1), b)
            lhs[pl.ds(pair * 256, 128), pl.ds(k * 128, 128)] = even.astype(bf16)
            lhs[pl.ds(pair * 256 + 128, 128), pl.ds(k * 128, 128)] = odd.astype(bf16)
    for i in (0, 1, -1, 2):
        spread.last(i)

    coeffs = meta[...]
    weights = [coeffs[:, j : j + 1] + coeffs[:, j + 4 : j + 5] + coeffs[:, j + 8 : j + 9] for j in range(4)]
    tops, bottoms = [], []
    for t in range(4):
        span = pl.ds(t * 256, 256)
        products = dot(lhs[...], points[:, :, :, span].reshape(1024, 256))
        scaled = products * (1.0 / 32.0)
        squared = scaled * scaled
        values = 0.25 * squared * squared
        line = jnp.zeros((128, 256), f32)
        for j in range(4):
            line = line + weights[j] * values[j * 128 : (j + 1) * 128]
        design_ref[:, span] = line
        largest = jnp.maximum(jnp.max(jnp.abs(line), axis=0, keepdims=True), 1e-30)
        exponent = jnp.floor(jnp.log2(largest)) - 14.0
        mantissa = jnp.minimum(jnp.ceil(largest * jnp.exp2(-exponent)), 32767.0)
        coded = line * (32767.0 / (mantissa * jnp.exp2(exponent)))
        for u in range(2):
            j = 2 * t + u
            part = as_i16(coded[:, 128 * u : 128 * u + 128])
            for half in (0, 1):
                buf[0, r, half, pl.ds(64 * j, 64), :] = part[64 * half : 64 * half + 64]
            tops.append(exponent[:, 128 * u : 128 * u + 128])
            bottoms.append(mantissa[:, 128 * u : 128 * u + 128])
    tile = as_i16(jnp.concatenate(tops + bottoms, axis=0))
    buf[0, r, 0, pl.ds(512, 16), :] = tile
    buf[0, r, 1, pl.ds(512, 16), :] = tile

    def panel_view(block, half, q):
        ref = buf.at[0, block, half]
        if q is None:
            return ref
        return ref.at[pl.ds(0, CUT)] if q == 0 else ref.at[pl.ds(CUT, HALF - CUT)]

    gather = TorusGather(x, y, panel_view, sends, recvs)
    gather.start()

    def z_copy(block, half, target, n, k):
        return pltpu.make_async_remote_copy(
            src_ref=buf.at[jnp.where(root, 0, 1), block, half],
            dst_ref=buf.at[1, block, half],
            send_sem=zsends.at[n, k],
            recv_sem=zrecvs.at[n, half],
            device_id=target,
            device_id_type=MESH,
        )

    def z_wait(block, half, n):
        ref = buf.at[1, block, half]
        pltpu.make_async_copy(ref, ref, zrecvs.at[n, half]).wait()

    hops = jnp.where(c == 0, dz, (8 - dz) % 8)
    not_end = hops != 7

    def pass_on(n):
        @pl.when(root)
        def _():
            for half in (0, 1):
                block = block_of(x, y, half, n)
                z_copy(block, half, up if half == 0 else down, n, half).start()
                z_copy(block, half, other, n, half + 2).start()

        for half in (0, 1):
            @pl.when(jnp.logical_and(jnp.logical_not(root_chip), c == half))
            def _():
                block = block_of(x, y, half, n)
                z_wait(block, half, n)

                @pl.when(not_end)
                def _():
                    z_copy(block, half, up if half == 0 else down, n, 0).start()

                z_copy(block, half, other, n, 1).start()

    def drained(n):
        ref = buf.at[0, 0, 0]

        @pl.when(root)
        def _():
            for k in range(4):
                pltpu.make_async_copy(ref, ref, zsends.at[n, k]).wait()

        @pl.when(jnp.logical_not(root_chip))
        def _():
            @pl.when(not_end)
            def _():
                pltpu.make_async_copy(ref, ref, zsends.at[n, 0]).wait()

            pltpu.make_async_copy(ref, ref, zsends.at[n, 1]).wait()

    from_root = jnp.where(root, 0, 1)

    def decode(half, u):
        for v in (0, 1):
            blocks = [block_of(x, y, half, 4 * u + 2 * v + k) for k in (0, 1)]

            @pl.when(jnp.logical_and(jnp.logical_not(root), jnp.logical_or(root_chip, c != half)))
            def _():
                for k in (0, 1):
                    z_wait(blocks[k], half, 4 * u + 2 * v + k)

            scale_p = [column_scale(buf[0, b, half, pl.ds(512, 16), :], 2.0 ** -11) for b in blocks]
            scale_r = [column_scale(buf[from_root, b, half, pl.ds(512, 16), :], 1.0) for b in blocks]
            for j in range(8):
                span = slice(128 * j, 128 * j + 128)
                piece = pl.ds(64 * j, 64)
                both_p = jnp.concatenate([
                    buf[0, b, half, piece, :].astype(jnp.int32).astype(f32) * scale[j : j + 1, :]
                    for b, scale in zip(blocks, scale_p)
                ], axis=0)
                spot = pl.ds(v * 128, 128)
                hp[half, spot, span], lp[half, spot, span] = split_bf16(both_p)
                both_r = jnp.concatenate([
                    buf[from_root, b, half, piece, :].astype(jnp.int32).astype(f32) * scale[j : j + 1, :]
                    for b, scale in zip(blocks, scale_r)
                ], axis=0)
                hrt[half, span, spot], lrt[half, span, spot] = split_bf16(both_r.T)

    def multiply(half, t):
        span = pl.ds(pl.multiple_of(t * 256, 256), 256)
        high = hrt[half]
        left = jnp.concatenate([high, high, lrt[half]], axis=1)
        right_high = hp[half, :, span]
        right = jnp.concatenate([right_high, lp[half, :, span], right_high], axis=0)
        out_ref[:, span] += dot(left, right)

    events = {
        2: gather.first, 5: lambda: gather.across(0), 6: gather.far, 8: lambda: gather.across(1),
        10: lambda: gather.across(-1), 12: lambda: gather.last(0), 13: lambda: gather.across(2),
        15: lambda: gather.last(1), 16: lambda: gather.last(-1), 17: lambda: gather.last(2),
    }

    @pl.loop(FIRST_SLOT, FIRST_SLOT + 16 + 13 + 8)
    def _(s):
        for slot, event in events.items():
            pl.when(s == slot)(event)
        n = s - FIRST_SLOT - hop_slots(hops)

        @pl.when(jnp.logical_and(n >= 0, n < 16))
        def _():
            pass_on(n)

        @pl.loop(0, 2)
        def _(half):
            steps = hop_slots(jnp.where(half == 0, dz, (8 - dz) % 8))
            late = jnp.where(jnp.logical_or(root, jnp.logical_and(half == c, jnp.logical_not(root_chip))), 0, 1)
            m = s - FIRST_SLOT - steps - late - 3

            @pl.when(jnp.logical_and(m >= 0, m < 16))
            def _():
                @pl.when(m % 4 == 0)
                def _():
                    decode(half, m // 4)

                multiply(half, m % 4)

    spread.drain()
    gather.drain()
    for k, (dx, dy) in enumerate(PLANE):
        post(k, dx, dy).wait_send()
    for n in range(3):
        feat_wait(0, fsend.at[n])
    for k in (1, 2, 3):
        for d in (1, -1):
            n = 3 + 4 * (k - 1) + (0 if d == 1 else 2)
            feat_wait(0, fsend.at[n], 0 if k == 3 else None)
            feat_wait(0, fsend.at[n + 1])
    feat_wait(0, fsend.at[15])

    @pl.loop(0, 16)
    def _(n):
        drained(n)


def on_device(env_desc, point_desc, pool_index, pool_count, pool_weight, row_dest):
    sem = pltpu.SemaphoreType.DMA
    return pl.pallas_call(
        whole_kernel,
        out_shape=(jax.ShapeDtypeStruct((128, 1024), f32), jax.ShapeDtypeStruct((1024, 1024), f32)),
        in_specs=[pl.BlockSpec(memory_space=VMEM)] * 6,
        out_specs=(pl.BlockSpec(memory_space=VMEM), pl.BlockSpec(memory_space=VMEM)),
        scratch_shapes=[
            VMEM((16, 2, 32, 1024), bf16),
            VMEM((16, 48, 128), bf16),
            VMEM((16, 48, 128), bf16),
            VMEM((16, 2, 128, 128), bf16),
            VMEM((128, 128), f32),
            VMEM((512, 1024), bf16),
            VMEM((2, 16, 2, HALF, 128), i16),
            VMEM((2, 256, 1024), bf16),
            VMEM((2, 256, 1024), bf16),
            VMEM((2, 1024, 256), bf16),
            VMEM((2, 1024, 256), bf16),
            sem((40,)), sem((40,)), sem((15,)), sem((15,)), sem(()), sem((16,)), sem((8,)), sem((8,)),
            sem((40,)), sem((40,)), sem((16, 4)), sem((16, 2)),
        ],
        compiler_params=pltpu.CompilerParams(collective_id=1, has_side_effects=True, vmem_limit_bytes=56 << 20),
        name="whole",
    )(env_desc, point_desc, pool_index, pool_count.reshape(256, 1), pool_weight, row_dest.reshape(256, 1))


def solution(mesh):
    in_specs = (
        P("rows", "pts"),
        P("pts", "rows"),
        P("rows", None),
        P("rows"),
        P("rows", None),
        P("rows"),
    )
    out_specs = (P("rows", "pts"), P("rows", "pts"))
    return jax.shard_map(
        on_device, mesh=mesh, in_specs=in_specs, out_specs=out_specs, check_vma=False
    )
```

```python
import jax
import jax.numpy as jnp
from jax import lax
from jax.experimental import pallas as pl
from jax.experimental.pallas import tpu as pltpu
from jax.sharding import PartitionSpec as P

damping = 0.5
MESH = pl.DeviceIdType.MESH
f32, bf16, i16 = jnp.float32, jnp.bfloat16, jnp.int16
HALF = 528
CUT = 256
VMEM = pltpu.VMEM


def split_bf16(value):
    high = value.astype(bf16)
    return high, (value - high.astype(f32)).astype(bf16)


def where_am_i():
    r = lax.axis_index("rows")
    p = lax.axis_index("pts")
    return r // 4, r % 4, p // 2, p % 2


def plane_id(x, y, dx, dy):
    return ((x + dx + 4) % 4) * 4 + (y + dy + 4) % 4


def gather_keys():
    keys = []
    for half in (0, 1):
        for i in (0, 1, -1, 2):
            for j in (0, 1, -1, 2):
                if (i, j) == (0, 0):
                    continue
                two = j == 2 or (j == 0 and i == 2)
                keys += [(half, i, j, q) for q in ((0, 1) if two else (None,))]
    return {key: n for n, key in enumerate(keys)}


KEYS = gather_keys()


class TorusGather:
    def __init__(self, x, y, view, send_sems, recv_sems):
        self.x, self.y, self.view = x, y, view
        self.send_sems, self.recv_sems = send_sems, recv_sems
        self.sends = 0

    def offset(self, half, a, b):
        return (a, b) if half == 0 else (b, a)

    def block(self, half, i, j):
        return plane_id(self.x, self.y, *self.offset(half, i, j))

    def copy(self, half, i, j, q, to, key):
        target = plane_id(self.x, self.y, *self.offset(half, *to))
        block = self.block(half, i, j)
        pltpu.make_async_remote_copy(
            src_ref=self.view(block, half, q),
            dst_ref=self.view(block, half, q),
            send_sem=self.send_sems.at[self.sends],
            recv_sem=self.recv_sems.at[KEYS[key]],
            device_id={"rows": target},
            device_id_type=MESH,
        ).start()
        self.sends += 1

    def wait(self, half, i, j, q):
        ref = self.view(self.block(half, i, j), half, q)
        pltpu.make_async_copy(ref, ref, self.recv_sems.at[KEYS[(half, i, j, q)]]).wait()

    def start(self):
        for half in (0, 1):
            for d in (1, -1):
                self.copy(half, 0, 0, None, (d, 0), (half, -d, 0, None))
        for half in (0, 1):
            for d in (1, -1):
                self.copy(half, 0, 0, None, (0, d), (half, 0, -d, None))

    def first(self):
        for half in (0, 1):
            for d in (1, -1):
                q = 0 if d == 1 else 1
                self.wait(half, -d, 0, None)
                self.copy(half, -d, 0, q, (d, 0), (half, 2, 0, q))
                for e in (1, -1):
                    self.copy(half, -d, 0, None, (0, e), (half, -d, -e, None))

    def across(self, i):
        for half in (0, 1):
            for d in (1, -1):
                q = 0 if d == 1 else 1
                self.wait(half, i, -d, None)
                self.copy(half, i, -d, q, (0, d), (half, i, 2, q))

    def far(self):
        for half in (0, 1):
            for q in (0, 1):
                self.wait(half, 2, 0, q)
            for e in (1, -1):
                self.copy(half, 2, 0, None, (0, e), (half, 2, -e, None))

    def last(self, i):
        for half in (0, 1):
            for q in (0, 1):
                self.wait(half, i, 2, q)

    def drain(self):
        n = 0
        for whole in self.order():
            ref = self.view(0, 0, whole)
            pltpu.make_async_copy(ref, ref, self.send_sems.at[n]).wait()
            n += 1

    def order(self):
        sizes = [None] * 8
        for half in (0, 1):
            for d in (1, -1):
                sizes += [0 if d == 1 else 1, None, None]
        sizes += [0, 1] * 2
        sizes += [None] * 4
        sizes += [0, 1] * 2
        sizes += [0, 1] * 2
        sizes += [0, 1] * 2
        return sizes


ORDER = [(0, 0), (1, 0), (-1, 0), (0, 1), (0, -1), (2, 0), (1, 1), (1, -1), (-1, 1), (-1, -1),
         (0, 2), (2, 1), (2, -1), (1, 2), (-1, 2), (2, 2)]
FIRST_SLOT = 2
SLOTS = 50


def signed(value):
    return value - (1 << 32) if value >= 1 << 31 else value


FIRST_STEPS = signed(sum((a % 4) << (2 * n) for n, (a, b) in enumerate(ORDER)))
SECOND_STEPS = signed(sum((b % 4) << (2 * n) for n, (a, b) in enumerate(ORDER)))
PLANE = [(dx, dy) for dx in range(4) for dy in range(4) if (dx, dy) != (0, 0)]


def block_of(x, y, half, n):
    a = (jnp.int32(FIRST_STEPS) >> (2 * n)) & 3
    b = (jnp.int32(SECOND_STEPS) >> (2 * n)) & 3
    dx = jnp.where(half == 0, a, b)
    dy = jnp.where(half == 0, b, a)
    return ((x + dx) % 4) * 4 + (y + dy) % 4


def hop_slots(hops):
    return (7 * hops + 3) // 4


def column_scale(tile, factor):
    parts = tile.astype(jnp.int32).astype(f32)
    return jnp.exp2(parts[:8]) * (parts[8:] * (factor / 32767.0))


def as_i16(value):
    return jnp.clip(jnp.round(value), -32767.0, 32767.0).astype(jnp.int32).astype(i16)


def iota(shape, axis):
    return lax.broadcasted_iota(jnp.int32, shape, axis)


def one_hot(test):
    return jnp.where(test, 1.0, 0.0).astype(bf16)


def dot(a, b, ca=1, cb=0):
    return lax.dot_general(a, b, (((ca,), (cb,)), ((), ())), preferred_element_type=f32)


def fill_outbox(env_ref, index_ref, count_ref, weight_ref, dest_ref, outbox):
    row = dest_ref[...]
    live = row >= 0
    dest = row >> 7
    owner = jnp.where(dest == iota((16, 256), 0), 1.0, 0.0)
    earlier = dot(owner.astype(bf16), one_hot(iota((256, 256), 0) < iota((256, 256), 1)))
    rank = jnp.sum(earlier * owner, axis=0, keepdims=True)
    place = jnp.where(live, dest.astype(f32) * 16.0 + rank, 999.0)
    move = one_hot(place == iota((256, 256), 0).astype(f32))
    env = env_ref[...]
    index = index_ref[...]
    envs = iota((512, 256), 0)
    picked = [dot(env, one_hot(index[j : j + 1] == envs)).astype(bf16) for j in range(4)]
    rest = jnp.where(iota((4, 256), 0) < count_ref[...], weight_ref[...], 0.0)
    meta = []
    for _ in range(3):
        part = rest.astype(bf16).astype(f32)
        rest = rest - part
        meta.append(part)
    within = jnp.where(live, (row & 127) + 1, 0).astype(f32)
    meta.append(jnp.where(iota((4, 256), 0) == 0, within, 0.0))
    meta.append(jnp.zeros((112, 256), f32))
    everything = jnp.concatenate(picked + [jnp.concatenate(meta, axis=0).astype(bf16)], axis=0)
    moved = dot(move, everything, 1, 1).astype(bf16)
    for d in range(16):
        for k in range(3):
            outbox[d, 16 * k : 16 * k + 16, :] = moved[16 * d : 16 * d + 16, 128 * k : 128 * k + 128]


def whole_kernel(env_ref, desc_ref, index_ref, count_ref, weight_ref, dest_ref, design_ref, out_ref,
                 points, outbox, inbox, feats, meta, lhs, buf, hp, lp, hrt, lrt,
                 psend, precv, osend, orecv, own_sem, fsend, frecv, frecv2, sends, recvs, zsends, zrecvs):
    x, y, z, c = where_am_i()
    r = x * 4 + y
    p = z * 2 + c
    z0, c0 = r // 2, r % 2
    dz = (z - z0 + 8) % 8
    root_chip = dz == 0
    root = jnp.logical_and(root_chip, c == c0)
    up = {"pts": ((z + 1) % 8) * 2}
    down = {"pts": ((z + 7) % 8) * 2 + 1}
    other = {"pts": z * 2 + 1 - c}
    along = {1: {"pts": ((z + 1) % 8) * 2 + c}, -1: {"pts": ((z + 7) % 8) * 2 + c}}
    beyond = {1: {"pts": ((z + 2) % 8) * 2 + c}, -1: {"pts": ((z + 6) % 8) * 2 + c}}
    barrier = pltpu.get_barrier_semaphore()
    for dx, dy in PLANE:
        pl.semaphore_signal(barrier, inc=1, device_id={"rows": plane_id(x, y, dx, dy)}, device_id_type=MESH)
    for dc in (0, 1):
        for target in ((z + 1) % 8, (z + 7) % 8):
            pl.semaphore_signal(barrier, inc=1, device_id={"pts": target * 2 + dc}, device_id_type=MESH)
    for target in (other, beyond[1], beyond[-1]):
        pl.semaphore_signal(barrier, inc=1, device_id=target, device_id_type=MESH)

    points[r, 0] = desc_ref[:32]
    points[r, 1] = desc_ref[32:]
    fill_outbox(env_ref, index_ref, count_ref, weight_ref, dest_ref, outbox)
    pl.semaphore_wait(barrier, 22)

    def post(k, dx, dy):
        target = plane_id(x, y, dx, dy)
        return pltpu.make_async_remote_copy(
            src_ref=outbox.at[target], dst_ref=inbox.at[r], send_sem=osend.at[k], recv_sem=orecv.at[k],
            device_id={"rows": target}, device_id_type=MESH,
        )

    for k, (dx, dy) in enumerate(PLANE):
        post(k, dx, dy).start()
    own_copy = pltpu.make_async_copy(outbox.at[r], inbox.at[r], own_sem)
    own_copy.start()

    def points_view(block, half, q):
        return points.at[block, half] if q is None else points.at[block, half, pl.ds(16 * q, 16)]

    spread = TorusGather(x, y, points_view, psend, precv)
    spread.start()

    rows = r * 1024 + iota((128, 1024), 0)
    cols = p * 1024 + iota((128, 1024), 1)

    @pl.loop(0, 8)
    def _(m):
        out_ref[pl.ds(pl.multiple_of(m * 128, 128), 128), :] = jnp.where(rows + m * 128 == cols, damping, 0.0)

    spread.first()
    own_copy.wait()
    for k, (dx, dy) in enumerate(PLANE):
        ref = inbox.at[plane_id(x, y, -dx, -dy)]
        pltpu.make_async_copy(ref, ref, orecv.at[k]).wait()
    arrived = [jnp.concatenate([inbox[g, 16 * k : 16 * k + 16, :] for g in range(16)], axis=0) for k in range(3)]
    spots = arrived[2][:, 12:13].astype(f32)
    put = one_hot(spots == (iota((256, 128), 1) + 1).astype(f32))
    placed = dot(put, jnp.concatenate(arrived, axis=1), 0, 0)
    feats[p, 0] = placed[:, :128].astype(bf16)
    feats[p, 1] = placed[:, 128:256].astype(bf16)
    meta[...] = placed[:, 256:]

    def feat_copy(offset, pair, target, n, recv):
        ref = feats.at[((z + offset + 8) % 8) * 2 + c]
        if pair is not None:
            ref = ref.at[pair]
        return pltpu.make_async_remote_copy(
            src_ref=ref, dst_ref=ref, send_sem=fsend.at[n], recv_sem=recv, device_id=target, device_id_type=MESH
        )

    def feat_wait(owner, sem, pair=None):
        ref = feats.at[owner]
        if pair is not None:
            ref = ref.at[pair]
        pltpu.make_async_copy(ref, ref, sem).wait()

    for n, (target, recv) in enumerate((
        (along[1], frecv.at[0]), (along[-1], frecv.at[4]), (beyond[1], frecv.at[1]), (beyond[-1], frecv.at[5]),
        (other, frecv2.at[0]),
    )):
        feat_copy(0, None, target, n, recv).start()

    def feat_step(k):
        for d, base in ((1, 0), (-1, 4)):
            n = 4 * k + 1 + (0 if d == 1 else 2)
            feat_wait(((z - d * k + 8) % 8) * 2 + c, frecv.at[base + k - 1])
            if k < 3:
                pair = None if k == 1 else base // 4
                feat_copy(-d * k, pair, beyond[d], n, frecv.at[base + k + 1]).start()
            else:
                n = 12 if d == 1 else 13
            feat_copy(-d * k, None, other, n + 1, frecv2.at[(8 - d * k) % 8]).start()

    feat_step(1)
    spread.across(0)
    feat_step(2)
    spread.far()
    feat_step(3)
    spread.across(1)
    spread.across(-1)
    for d, base, pair in ((1, 0, 0), (-1, 4, 1)):
        feat_wait(((z + 4) % 8) * 2 + c, frecv.at[base + 3], pair)
    feat_copy(4, None, other, 15, frecv2.at[4]).start()
    for k in range(8):
        feat_wait(((z + k) % 8) * 2 + 1 - c, frecv2.at[k])
    spread.across(2)
    lane = iota((128, 128), 1)
    for k in range(8):
        for pair in (0, 1):
            a = feats[2 * k, pair].astype(f32)
            b = feats[2 * k + 1, pair].astype(f32)
            even = jnp.where(lane < 64, a, pltpu.roll(b, 64, 1))
            odd = jnp.where(lane < 64, pltpu.roll(a, 64, 1), b)
            lhs[pl.ds(pair * 256, 128), pl.ds(k * 128, 128)] = even.astype(bf16)
            lhs[pl.ds(pair * 256 + 128, 128), pl.ds(k * 128, 128)] = odd.astype(bf16)
    for i in (0, 1, -1, 2):
        spread.last(i)

    coeffs = meta[...]
    weights = [coeffs[:, j : j + 1] + coeffs[:, j + 4 : j + 5] + coeffs[:, j + 8 : j + 9] for j in range(4)]
    tops, bottoms = [], []
    for t in range(4):
        span = pl.ds(t * 256, 256)
        products = dot(lhs[...], points[:, :, :, span].reshape(1024, 256))
        scaled = products * (1.0 / 32.0)
        squared = scaled * scaled
        values = 0.25 * squared * squared
        line = jnp.zeros((128, 256), f32)
        for j in range(4):
            line = line + weights[j] * values[j * 128 : (j + 1) * 128]
        design_ref[:, span] = line
        largest = jnp.maximum(jnp.max(jnp.abs(line), axis=0, keepdims=True), 1e-30)
        exponent = jnp.floor(jnp.log2(largest)) - 14.0
        mantissa = jnp.minimum(jnp.ceil(largest * jnp.exp2(-exponent)), 32767.0)
        coded = line * (32767.0 / (mantissa * jnp.exp2(exponent)))
        for u in range(2):
            j = 2 * t + u
            part = as_i16(coded[:, 128 * u : 128 * u + 128])
            for half in (0, 1):
                buf[0, r, half, pl.ds(64 * j, 64), :] = part[64 * half : 64 * half + 64]
            tops.append(exponent[:, 128 * u : 128 * u + 128])
            bottoms.append(mantissa[:, 128 * u : 128 * u + 128])
    tile = as_i16(jnp.concatenate(tops + bottoms, axis=0))
    buf[0, r, 0, pl.ds(512, 16), :] = tile
    buf[0, r, 1, pl.ds(512, 16), :] = tile

    def panel_view(block, half, q):
        ref = buf.at[0, block, half]
        if q is None:
            return ref
        return ref.at[pl.ds(0, CUT)] if q == 0 else ref.at[pl.ds(CUT, HALF - CUT)]

    gather = TorusGather(x, y, panel_view, sends, recvs)
    gather.start()

    def z_copy(block, half, target, n, k):
        return pltpu.make_async_remote_copy(
            src_ref=buf.at[jnp.where(root, 0, 1), block, half],
            dst_ref=buf.at[1, block, half],
            send_sem=zsends.at[n, k],
            recv_sem=zrecvs.at[n, half],
            device_id=target,
            device_id_type=MESH,
        )

    def z_wait(block, half, n):
        ref = buf.at[1, block, half]
        pltpu.make_async_copy(ref, ref, zrecvs.at[n, half]).wait()

    hops = jnp.where(c == 0, dz, (8 - dz) % 8)
    not_end = hops != 7

    def pass_on(n):
        @pl.when(root)
        def _():
            for half in (0, 1):
                block = block_of(x, y, half, n)
                z_copy(block, half, up if half == 0 else down, n, half).start()
                z_copy(block, half, other, n, half + 2).start()

        for half in (0, 1):
            @pl.when(jnp.logical_and(jnp.logical_not(root_chip), c == half))
            def _():
                block = block_of(x, y, half, n)
                z_wait(block, half, n)

                @pl.when(not_end)
                def _():
                    z_copy(block, half, up if half == 0 else down, n, 0).start()

                z_copy(block, half, other, n, 1).start()

    def drained(n):
        ref = buf.at[0, 0, 0]

        @pl.when(root)
        def _():
            for k in range(4):
                pltpu.make_async_copy(ref, ref, zsends.at[n, k]).wait()

        @pl.when(jnp.logical_not(root_chip))
        def _():
            @pl.when(not_end)
            def _():
                pltpu.make_async_copy(ref, ref, zsends.at[n, 0]).wait()

            pltpu.make_async_copy(ref, ref, zsends.at[n, 1]).wait()

    from_root = jnp.where(root, 0, 1)

    def decode(half, u):
        for v in (0, 1):
            blocks = [block_of(x, y, half, 4 * u + 2 * v + k) for k in (0, 1)]

            @pl.when(jnp.logical_and(jnp.logical_not(root), jnp.logical_or(root_chip, c != half)))
            def _():
                for k in (0, 1):
                    z_wait(blocks[k], half, 4 * u + 2 * v + k)

            scale_p = [column_scale(buf[0, b, half, pl.ds(512, 16), :], 2.0 ** -11) for b in blocks]
            scale_r = [column_scale(buf[from_root, b, half, pl.ds(512, 16), :], 1.0) for b in blocks]
            for j in range(8):
                span = slice(128 * j, 128 * j + 128)
                piece = pl.ds(64 * j, 64)
                both_p = jnp.concatenate([
                    buf[0, b, half, piece, :].astype(jnp.int32).astype(f32) * scale[j : j + 1, :]
                    for b, scale in zip(blocks, scale_p)
                ], axis=0)
                spot = pl.ds(v * 128, 128)
                hp[half, spot, span], lp[half, spot, span] = split_bf16(both_p)
                both_r = jnp.concatenate([
                    buf[from_root, b, half, piece, :].astype(jnp.int32).astype(f32) * scale[j : j + 1, :]
                    for b, scale in zip(blocks, scale_r)
                ], axis=0)
                hrt[half, span, spot], lrt[half, span, spot] = split_bf16(both_r.T)

    def multiply(half, t):
        span = pl.ds(pl.multiple_of(t * 256, 256), 256)
        high = hrt[half]
        left = jnp.concatenate([high, high, lrt[half]], axis=1)
        right_high = hp[half, :, span]
        right = jnp.concatenate([right_high, lp[half, :, span], right_high], axis=0)
        out_ref[:, span] += dot(left, right)

    events = {
        2: gather.first, 5: lambda: gather.across(0), 6: gather.far, 8: lambda: gather.across(1),
        10: lambda: gather.across(-1), 12: lambda: gather.last(0), 13: lambda: gather.across(2),
        15: lambda: gather.last(1), 16: lambda: gather.last(-1), 17: lambda: gather.last(2),
    }

    @pl.loop(FIRST_SLOT, FIRST_SLOT + 16 + 13 + 8)
    def _(s):
        for slot, event in events.items():
            pl.when(s == slot)(event)
        n = s - FIRST_SLOT - hop_slots(hops)

        @pl.when(jnp.logical_and(n >= 0, n < 16))
        def _():
            pass_on(n)

        @pl.loop(0, 2)
        def _(half):
            steps = hop_slots(jnp.where(half == 0, dz, (8 - dz) % 8))
            late = jnp.where(jnp.logical_or(root, jnp.logical_and(half == c, jnp.logical_not(root_chip))), 0, 1)
            m = s - FIRST_SLOT - steps - late - 3

            @pl.when(jnp.logical_and(m >= 0, m < 16))
            def _():
                @pl.when(m % 4 == 0)
                def _():
                    decode(half, m // 4)

                multiply(half, m % 4)

    spread.drain()
    gather.drain()
    for k, (dx, dy) in enumerate(PLANE):
        post(k, dx, dy).wait_send()
    for n in range(16):
        feat_wait(0, fsend.at[n], 0 if n in (9, 11) else None)

    @pl.loop(0, 16)
    def _(n):
        drained(n)


def on_device(env_desc, point_desc, pool_index, pool_count, pool_weight, row_dest):
    sem = pltpu.SemaphoreType.DMA
    return pl.pallas_call(
        whole_kernel,
        out_shape=(pltpu.VMEM((128, 1024), f32), pltpu.VMEM((1024, 1024), f32)),
        in_specs=[pl.BlockSpec(memory_space=VMEM)] * 6,
        out_specs=(pl.BlockSpec(memory_space=VMEM), pl.BlockSpec(memory_space=VMEM)),
        scratch_shapes=[
            VMEM((16, 2, 32, 1024), bf16),
            VMEM((16, 48, 128), bf16),
            VMEM((16, 48, 128), bf16),
            VMEM((16, 2, 128, 128), bf16),
            VMEM((128, 128), f32),
            VMEM((512, 1024), bf16),
            VMEM((2, 16, 2, HALF, 128), i16),
            VMEM((2, 256, 1024), bf16),
            VMEM((2, 256, 1024), bf16),
            VMEM((2, 1024, 256), bf16),
            VMEM((2, 1024, 256), bf16),
            sem((40,)), sem((40,)), sem((15,)), sem((15,)), sem(()), sem((16,)), sem((8,)), sem((8,)),
            sem((40,)), sem((40,)), sem((16, 4)), sem((16, 2)),
        ],
        compiler_params=pltpu.CompilerParams(collective_id=1, has_side_effects=True, vmem_limit_bytes=56 << 20),
        name="whole",
    )(env_desc.T, point_desc.T, pool_index.T, pool_count.reshape(1, 256), pool_weight.T, row_dest.reshape(1, 256))


def solution(mesh):
    in_specs = (
        P("rows", "pts"),
        P("pts", "rows"),
        P("rows", None),
        P("rows"),
        P("rows", None),
        P("rows"),
    )
    out_specs = (P("rows", "pts"), P("rows", "pts"))
    return jax.shard_map(
        on_device, mesh=mesh, in_specs=in_specs, out_specs=out_specs, check_vma=False
    )
```

```python
import jax
import jax.numpy as jnp
from jax import lax
from jax.experimental import pallas as pl
from jax.experimental.pallas import tpu as pltpu
from jax.sharding import PartitionSpec as P

damping = 0.5
MESH = pl.DeviceIdType.MESH
f32, bf16, i16 = jnp.float32, jnp.bfloat16, jnp.int16
HALF = 528
CUT = 256
VMEM = pltpu.VMEM


def split_bf16(value):
    high = value.astype(bf16)
    return high, (value - high.astype(f32)).astype(bf16)


def where_am_i():
    r = lax.axis_index("rows")
    p = lax.axis_index("pts")
    return r // 4, r % 4, p // 2, p % 2


def plane_id(x, y, dx, dy):
    return ((x + dx + 4) % 4) * 4 + (y + dy + 4) % 4


def gather_keys():
    keys = []
    for half in (0, 1):
        for i in (0, 1, -1, 2):
            for j in (0, 1, -1, 2):
                if (i, j) == (0, 0):
                    continue
                two = j == 2 or (j == 0 and i == 2)
                keys += [(half, i, j, q) for q in ((0, 1) if two else (None,))]
    return {key: n for n, key in enumerate(keys)}


KEYS = gather_keys()


class TorusGather:
    def __init__(self, x, y, view, send_sems, recv_sems):
        self.x, self.y, self.view = x, y, view
        self.send_sems, self.recv_sems = send_sems, recv_sems
        self.sends = 0

    def offset(self, half, a, b):
        return (a, b) if half == 0 else (b, a)

    def block(self, half, i, j):
        return plane_id(self.x, self.y, *self.offset(half, i, j))

    def copy(self, half, i, j, q, to, key):
        target = plane_id(self.x, self.y, *self.offset(half, *to))
        block = self.block(half, i, j)
        pltpu.make_async_remote_copy(
            src_ref=self.view(block, half, q),
            dst_ref=self.view(block, half, q),
            send_sem=self.send_sems.at[self.sends],
            recv_sem=self.recv_sems.at[KEYS[key]],
            device_id={"rows": target},
            device_id_type=MESH,
        ).start()
        self.sends += 1

    def wait(self, half, i, j, q):
        ref = self.view(self.block(half, i, j), half, q)
        pltpu.make_async_copy(ref, ref, self.recv_sems.at[KEYS[(half, i, j, q)]]).wait()

    def start(self):
        for half in (0, 1):
            for d in (1, -1):
                self.copy(half, 0, 0, None, (d, 0), (half, -d, 0, None))
        for half in (0, 1):
            for d in (1, -1):
                self.copy(half, 0, 0, None, (0, d), (half, 0, -d, None))

    def first(self):
        for half in (0, 1):
            for d in (1, -1):
                q = 0 if d == 1 else 1
                self.wait(half, -d, 0, None)
                self.copy(half, -d, 0, q, (d, 0), (half, 2, 0, q))
                for e in (1, -1):
                    self.copy(half, -d, 0, None, (0, e), (half, -d, -e, None))

    def across(self, i):
        for half in (0, 1):
            for d in (1, -1):
                q = 0 if d == 1 else 1
                self.wait(half, i, -d, None)
                self.copy(half, i, -d, q, (0, d), (half, i, 2, q))

    def far(self):
        for half in (0, 1):
            for q in (0, 1):
                self.wait(half, 2, 0, q)
            for e in (1, -1):
                self.copy(half, 2, 0, None, (0, e), (half, 2, -e, None))

    def last(self, i):
        for half in (0, 1):
            for q in (0, 1):
                self.wait(half, i, 2, q)

    def drain(self):
        n = 0
        for whole in self.order():
            ref = self.view(0, 0, whole)
            pltpu.make_async_copy(ref, ref, self.send_sems.at[n]).wait()
            n += 1

    def order(self):
        sizes = [None] * 8
        for half in (0, 1):
            for d in (1, -1):
                sizes += [0 if d == 1 else 1, None, None]
        sizes += [0, 1] * 2
        sizes += [None] * 4
        sizes += [0, 1] * 2
        sizes += [0, 1] * 2
        sizes += [0, 1] * 2
        return sizes


PLANE = [(dx, dy) for dx in range(4) for dy in range(4) if (dx, dy) != (0, 0)]


def column_scale(tile, factor):
    parts = tile.astype(jnp.int32).astype(f32)
    return jnp.exp2(parts[:8]) * (parts[8:] * (factor / 32767.0))


def as_i16(value):
    return jnp.clip(jnp.round(value), -32767.0, 32767.0).astype(jnp.int32).astype(i16)


def iota(shape, axis):
    return lax.broadcasted_iota(jnp.int32, shape, axis)


def one_hot(test):
    return jnp.where(test, 1.0, 0.0).astype(bf16)


def dot(a, b, ca=1, cb=0):
    return lax.dot_general(a, b, (((ca,), (cb,)), ((), ())), preferred_element_type=f32)


def fill_outbox(env_ref, index_ref, count_ref, weight_ref, dest_ref, outbox):
    row = dest_ref[...]
    live = row >= 0
    dest = row >> 7
    owner = jnp.where(dest == iota((16, 256), 0), 1.0, 0.0)
    earlier = dot(owner.astype(bf16), one_hot(iota((256, 256), 0) < iota((256, 256), 1)))
    rank = jnp.sum(earlier * owner, axis=0, keepdims=True)
    place = jnp.where(live, dest.astype(f32) * 16.0 + rank, 999.0)
    move = one_hot(place == iota((256, 256), 0).astype(f32))
    env = env_ref[...]
    index = index_ref[...]
    envs = iota((512, 256), 0)
    picked = [dot(env, one_hot(index[j : j + 1] == envs)).astype(bf16) for j in range(4)]
    rest = jnp.where(iota((4, 256), 0) < count_ref[...], weight_ref[...], 0.0)
    meta = []
    for _ in range(3):
        part = rest.astype(bf16).astype(f32)
        rest = rest - part
        meta.append(part)
    within = jnp.where(live, (row & 127) + 1, 0).astype(f32)
    meta.append(jnp.where(iota((4, 256), 0) == 0, within, 0.0))
    meta.append(jnp.zeros((112, 256), f32))
    everything = jnp.concatenate(picked + [jnp.concatenate(meta, axis=0).astype(bf16)], axis=0)
    moved = dot(move, everything, 1, 1).astype(bf16)
    for d in range(16):
        for k in range(3):
            outbox[d, 16 * k : 16 * k + 16, :] = moved[16 * d : 16 * d + 16, 128 * k : 128 * k + 128]


def whole_kernel(env_ref, desc_ref, index_ref, count_ref, weight_ref, dest_ref, design_ref, out_ref,
                 points, outbox, inbox, feats, meta, lhs, buf, hp, lp, hrt, lrt,
                 psend, precv, osend, orecv, own_sem, fsend, frecv, frecv2, sends, recvs, middle, rsend, rrecv, tsend, trecv, zsend, zrecv, zsend2, zrecv2):
    x, y, z, c = where_am_i()
    r = x * 4 + y
    p = z * 2 + c
    lift = (7 * p + 16 - r) % 16
    drop = (7 * (p + r)) % 16
    source = (7 * r + 16 - p) % 16
    lifts, drops = lift != p, drop != r
    other = {"pts": z * 2 + 1 - c}
    along = {1: {"pts": ((z + 1) % 8) * 2 + c}, -1: {"pts": ((z + 7) % 8) * 2 + c}}
    beyond = {1: {"pts": ((z + 2) % 8) * 2 + c}, -1: {"pts": ((z + 6) % 8) * 2 + c}}
    barrier = pltpu.get_barrier_semaphore()
    for dx, dy in PLANE:
        pl.semaphore_signal(barrier, inc=1, device_id={"rows": plane_id(x, y, dx, dy)}, device_id_type=MESH)
    for d in (1, -1):
        pl.semaphore_signal(barrier, inc=1, device_id=along[d], device_id_type=MESH)

    for moves, targets in ((lifts, ({"pts": lift}, {"pts": drop})), (drops, ({"rows": drop}, {"rows": source}))):
        @pl.when(moves)
        def _():
            for target in targets:
                pl.semaphore_signal(barrier, inc=1, device_id=target, device_id_type=MESH)

    for target in (other, beyond[1], beyond[-1]):
        pl.semaphore_signal(barrier, inc=1, device_id=target, device_id_type=MESH)

    points[r, 0] = desc_ref[:32]
    points[r, 1] = desc_ref[32:]
    fill_outbox(env_ref, index_ref, count_ref, weight_ref, dest_ref, outbox)
    pl.semaphore_wait(barrier, 20 + jnp.where(lifts, 2, 0) + jnp.where(drops, 2, 0))

    def post(k, dx, dy):
        target = plane_id(x, y, dx, dy)
        return pltpu.make_async_remote_copy(
            src_ref=outbox.at[target], dst_ref=inbox.at[r], send_sem=osend.at[k], recv_sem=orecv.at[k],
            device_id={"rows": target}, device_id_type=MESH,
        )

    for k, (dx, dy) in enumerate(PLANE):
        post(k, dx, dy).start()
    own_copy = pltpu.make_async_copy(outbox.at[r], inbox.at[r], own_sem)
    own_copy.start()

    def points_view(block, half, q):
        return points.at[block, half] if q is None else points.at[block, half, pl.ds(16 * q, 16)]

    spread = TorusGather(x, y, points_view, psend, precv)
    spread.start()

    rows = r * 1024 + iota((128, 1024), 0)
    cols = p * 1024 + iota((128, 1024), 1)

    @pl.loop(0, 8)
    def _(m):
        out_ref[pl.ds(pl.multiple_of(m * 128, 128), 128), :] = jnp.where(rows + m * 128 == cols, damping, 0.0)

    spread.first()
    own_copy.wait()
    for k, (dx, dy) in enumerate(PLANE):
        ref = inbox.at[plane_id(x, y, -dx, -dy)]
        pltpu.make_async_copy(ref, ref, orecv.at[k]).wait()
    arrived = [jnp.concatenate([inbox[g, 16 * k : 16 * k + 16, :] for g in range(16)], axis=0) for k in range(3)]
    spots = arrived[2][:, 12:13].astype(f32)
    put = one_hot(spots == (iota((256, 128), 1) + 1).astype(f32))
    placed = dot(put, jnp.concatenate(arrived, axis=1), 0, 0)
    feats[p, 0] = placed[:, :128].astype(bf16)
    feats[p, 1] = placed[:, 128:256].astype(bf16)
    meta[...] = placed[:, 256:]

    def feat_copy(offset, pair, target, n, recv):
        ref = feats.at[((z + offset + 8) % 8) * 2 + c]
        if pair is not None:
            ref = ref.at[pair]
        return pltpu.make_async_remote_copy(
            src_ref=ref, dst_ref=ref, send_sem=fsend.at[n], recv_sem=recv, device_id=target, device_id_type=MESH
        )

    def feat_wait(owner, sem, pair=None):
        ref = feats.at[owner]
        if pair is not None:
            ref = ref.at[pair]
        pltpu.make_async_copy(ref, ref, sem).wait()

    for n, (target, recv) in enumerate((
        (along[1], frecv.at[0]), (along[-1], frecv.at[4]), (beyond[1], frecv.at[1]), (beyond[-1], frecv.at[5]),
        (other, frecv2.at[0]),
    )):
        feat_copy(0, None, target, n, recv).start()

    def feat_step(k):
        for d, base in ((1, 0), (-1, 4)):
            n = 4 * k + 1 + (0 if d == 1 else 2)
            feat_wait(((z - d * k + 8) % 8) * 2 + c, frecv.at[base + k - 1])
            if k < 3:
                pair = None if k == 1 else base // 4
                feat_copy(-d * k, pair, beyond[d], n, frecv.at[base + k + 1]).start()
            else:
                n = 12 if d == 1 else 13
            feat_copy(-d * k, None, other, n + 1, frecv2.at[(8 - d * k) % 8]).start()

    feat_step(1)
    spread.across(0)
    feat_step(2)
    spread.far()
    feat_step(3)
    spread.across(1)
    spread.across(-1)
    for d, base, pair in ((1, 0, 0), (-1, 4, 1)):
        feat_wait(((z + 4) % 8) * 2 + c, frecv.at[base + 3], pair)
    feat_copy(4, None, other, 15, frecv2.at[4]).start()
    for k in range(8):
        feat_wait(((z + k) % 8) * 2 + 1 - c, frecv2.at[k])
    spread.across(2)
    lane = iota((128, 128), 1)
    for k in range(8):
        for pair in (0, 1):
            a = feats[2 * k, pair].astype(f32)
            b = feats[2 * k + 1, pair].astype(f32)
            even = jnp.where(lane < 64, a, pltpu.roll(b, 64, 1))
            odd = jnp.where(lane < 64, pltpu.roll(a, 64, 1), b)
            lhs[pl.ds(pair * 256, 128), pl.ds(k * 128, 128)] = even.astype(bf16)
            lhs[pl.ds(pair * 256 + 128, 128), pl.ds(k * 128, 128)] = odd.astype(bf16)
    for i in (0, 1, -1, 2):
        spread.last(i)

    coeffs = meta[...]
    weights = [coeffs[:, j : j + 1] + coeffs[:, j + 4 : j + 5] + coeffs[:, j + 8 : j + 9] for j in range(4)]
    tops, bottoms = [], []
    for t in range(4):
        span = pl.ds(t * 256, 256)
        products = dot(lhs[...], points[:, :, :, span].reshape(1024, 256))
        scaled = products * (1.0 / 32.0)
        squared = scaled * scaled
        values = 0.25 * squared * squared
        line = jnp.zeros((128, 256), f32)
        for j in range(4):
            line = line + weights[j] * values[j * 128 : (j + 1) * 128]
        design_ref[:, span] = line
        largest = jnp.maximum(jnp.max(jnp.abs(line), axis=0, keepdims=True), 1e-30)
        exponent = jnp.floor(jnp.log2(largest)) - 14.0
        mantissa = jnp.minimum(jnp.ceil(largest * jnp.exp2(-exponent)), 32767.0)
        coded = line * (32767.0 / (mantissa * jnp.exp2(exponent)))
        for u in range(2):
            j = 2 * t + u
            part = as_i16(coded[:, 128 * u : 128 * u + 128])
            for half in (0, 1):
                buf[0, r, half, pl.ds(64 * j, 64), :] = part[64 * half : 64 * half + 64]
            tops.append(exponent[:, 128 * u : 128 * u + 128])
            bottoms.append(mantissa[:, 128 * u : 128 * u + 128])
    tile = as_i16(jnp.concatenate(tops + bottoms, axis=0))
    buf[0, r, 0, pl.ds(512, 16), :] = tile
    buf[0, r, 1, pl.ds(512, 16), :] = tile

    def panel_view(block, half, q):
        ref = buf.at[0, block, half]
        if q is None:
            return ref
        return ref.at[pl.ds(0, CUT)] if q == 0 else ref.at[pl.ds(CUT, HALF - CUT)]

    def rise(half):
        return pltpu.make_async_remote_copy(
            src_ref=buf.at[0, r, half], dst_ref=middle.at[half], send_sem=rsend.at[half], recv_sem=rrecv.at[half],
            device_id={"pts": lift}, device_id_type=MESH,
        )

    def turn(half):
        return pltpu.make_async_remote_copy(
            src_ref=middle.at[half], dst_ref=buf.at[1, p, half], send_sem=tsend.at[half], recv_sem=trecv.at[half],
            device_id={"rows": drop}, device_id_type=MESH,
        )

    for half in (0, 1):
        pl.when(lifts)(lambda: rise(half).start())
        pl.when(jnp.logical_not(lifts))(
            lambda: pltpu.make_async_copy(buf.at[0, r, half], middle.at[half], rrecv.at[half]).start()
        )

    gather = TorusGather(x, y, panel_view, sends, recvs)
    gather.start()

    def ring_copy(offset, half, target, send, recv):
        ref = buf.at[1, ((z + offset + 8) % 8) * 2 + c, half]
        return pltpu.make_async_remote_copy(
            src_ref=ref, dst_ref=ref, send_sem=send, recv_sem=recv, device_id=target, device_id_type=MESH
        )

    def half_wait(owner, half, sem):
        ref = buf.at[1, owner, half]
        pltpu.make_async_copy(ref, ref, sem).wait()

    def ring_step(k):
        for half in (0, 1):
            for d, side in ((1, 0), (-1, 1)):
                if k == 4 and half != side:
                    continue
                if k == 0:
                    if d == 1:
                        half_wait(p, half, trecv.at[half])
                else:
                    half_wait(((z - d * k + 8) % 8) * 2 + c, half, zrecv.at[side, k - 1, half])
                if k < 3 or (k == 3 and half == side):
                    ring_copy(-d * k, half, along[d], zsend.at[side, k, half], zrecv.at[side, k, half]).start()
                if k > 0 or d == 1:
                    o = (8 - d * k) % 8
                    ring_copy(o, half, other, zsend2.at[o, half], zrecv2.at[o, half]).start()

    def compute(o):
        zz = (z + o + 8) % 8
        for half in (0, 1):
            half_wait(2 * zz + 1 - c, half, zrecv2.at[(o + 8) % 8, half])
        for v in (0, 1):
            b, slot = (7 * r + 32 - 2 * zz - v) % 16, 2 * zz + v
            scale_p = column_scale(buf[0, b, 0, pl.ds(512, 16), :], 2.0 ** -11)
            scale_r = column_scale(buf[1, slot, 0, pl.ds(512, 16), :], 1.0)
            spot = pl.ds(v * 128, 128)
            for j in range(8):
                span = slice(128 * j, 128 * j + 128)
                both = [
                    jnp.concatenate([buf[k, at, half, pl.ds(64 * j, 64), :] for half in (0, 1)], axis=0)
                    .astype(jnp.int32).astype(f32) * scale[j : j + 1, :]
                    for k, at, scale in ((0, b, scale_p), (1, slot, scale_r))
                ]
                hp[spot, span], lp[spot, span] = split_bf16(both[0])
                hrt[span, spot], lrt[span, spot] = split_bf16(both[1].T)

        @pl.loop(0, 4)
        def _(t):
            span = pl.ds(pl.multiple_of(t * 256, 256), 256)
            high = hrt[...]
            left = jnp.concatenate([high, high, lrt[...]], axis=1)
            right_high = hp[:, span]
            right = jnp.concatenate([right_high, lp[:, span], right_high], axis=0)
            out_ref[:, span] += dot(left, right)

    gather.first()
    for half in (0, 1):
        pltpu.make_async_copy(middle.at[half], middle.at[half], rrecv.at[half]).wait()
        pl.when(drops)(lambda: turn(half).start())
        pl.when(jnp.logical_not(drops))(
            lambda: pltpu.make_async_copy(middle.at[half], buf.at[1, p, half], trecv.at[half]).start()
        )
    gather.across(0)
    gather.far()
    ring_step(0)
    gather.across(1)
    gather.across(-1)
    gather.last(0)
    gather.across(2)
    ring_step(1)
    gather.last(1)
    gather.last(-1)
    gather.last(2)

    @pl.loop(0, 2)
    def _(i):
        compute(i)

    ring_step(2)

    @pl.loop(0, 2)
    def _(i):
        compute(3 * i - 1)

    ring_step(3)

    @pl.loop(0, 3)
    def _(i):
        compute(jnp.where(i == 0, -2, 9 - 6 * i))

    ring_step(4)
    compute(4)

    spread.drain()
    gather.drain()
    for k, (dx, dy) in enumerate(PLANE):
        post(k, dx, dy).wait_send()
    for n in range(16):
        feat_wait(0, fsend.at[n], 0 if n in (9, 11) else None)

    for half in (0, 1):
        pl.when(lifts)(lambda: rise(half).wait_send())
        pl.when(drops)(lambda: turn(half).wait_send())

    for half in (0, 1):
        for side in (0, 1):
            for k in range(4):
                if k < 3 or half == side:
                    half_wait(0, half, zsend.at[side, k, half])
        for o in range(8):
            half_wait(0, half, zsend2.at[o, half])


def on_device(env_desc, point_desc, pool_index, pool_count, pool_weight, row_dest):
    sem = pltpu.SemaphoreType.DMA
    return pl.pallas_call(
        whole_kernel,
        out_shape=(pltpu.VMEM((128, 1024), f32), pltpu.VMEM((1024, 1024), f32)),
        in_specs=[pl.BlockSpec(memory_space=VMEM)] * 6,
        out_specs=(pl.BlockSpec(memory_space=VMEM), pl.BlockSpec(memory_space=VMEM)),
        scratch_shapes=[
            VMEM((16, 2, 32, 1024), bf16),
            VMEM((16, 48, 128), bf16),
            VMEM((16, 48, 128), bf16),
            VMEM((16, 2, 128, 128), bf16),
            VMEM((128, 128), f32),
            VMEM((512, 1024), bf16),
            VMEM((2, 16, 2, HALF, 128), i16),
            VMEM((256, 1024), bf16),
            VMEM((256, 1024), bf16),
            VMEM((1024, 256), bf16),
            VMEM((1024, 256), bf16),
            sem((40,)), sem((40,)), sem((15,)), sem((15,)), sem(()), sem((16,)), sem((8,)), sem((8,)),
            sem((40,)), sem((40,)), VMEM((2, HALF, 128), i16),
            sem((2,)), sem((2,)), sem((2,)), sem((2,)), sem((2, 4, 2)), sem((2, 4, 2)), sem((8, 2)), sem((8, 2)),
        ],
        compiler_params=pltpu.CompilerParams(collective_id=1, has_side_effects=True, vmem_limit_bytes=56 << 20),
        name="whole",
    )(env_desc.T, point_desc.T, pool_index.T, pool_count.reshape(1, 256), pool_weight.T, row_dest.reshape(1, 256))


def solution(mesh):
    in_specs = (
        P("rows", "pts"),
        P("pts", "rows"),
        P("rows", None),
        P("rows"),
        P("rows", None),
        P("rows"),
    )
    out_specs = (P("rows", "pts"), P("rows", "pts"))
    return jax.shard_map(
        on_device, mesh=mesh, in_specs=in_specs, out_specs=out_specs, check_vma=False
    )
```

```python
import jax
import jax.numpy as jnp
from jax import lax
from jax.experimental import pallas as pl
from jax.experimental.pallas import tpu as pltpu
from jax.sharding import PartitionSpec as P

damping = 0.5
MESH = pl.DeviceIdType.MESH
f32, bf16, i16 = jnp.float32, jnp.bfloat16, jnp.int16
HALF = 528
CUT = 256
VMEM = pltpu.VMEM


def split_bf16(value):
    high = value.astype(bf16)
    return high, (value - high.astype(f32)).astype(bf16)


def where_am_i():
    r = lax.axis_index("rows")
    p = lax.axis_index("pts")
    return r // 4, r % 4, p // 2, p % 2


def plane_id(x, y, dx, dy):
    return ((x + dx + 4) % 4) * 4 + (y + dy + 4) % 4


def gather_keys():
    keys = []
    for half in (0, 1):
        for i in (0, 1, -1, 2):
            for j in (0, 1, -1, 2):
                if (i, j) == (0, 0):
                    continue
                two = j == 2 or (j == 0 and i == 2)
                keys += [(half, i, j, q) for q in ((0, 1) if two else (None,))]
    return {key: n for n, key in enumerate(keys)}


KEYS = gather_keys()


class TorusGather:
    def __init__(self, x, y, view, send_sems, recv_sems):
        self.x, self.y, self.view = x, y, view
        self.send_sems, self.recv_sems = send_sems, recv_sems
        self.sends = 0

    def offset(self, half, a, b):
        return (a, b) if half == 0 else (b, a)

    def block(self, half, i, j):
        return plane_id(self.x, self.y, *self.offset(half, i, j))

    def copy(self, half, i, j, q, to, key):
        target = plane_id(self.x, self.y, *self.offset(half, *to))
        block = self.block(half, i, j)
        pltpu.make_async_remote_copy(
            src_ref=self.view(block, half, q),
            dst_ref=self.view(block, half, q),
            send_sem=self.send_sems.at[self.sends],
            recv_sem=self.recv_sems.at[KEYS[key]],
            device_id={"rows": target},
            device_id_type=MESH,
        ).start()
        self.sends += 1

    def wait(self, half, i, j, q):
        ref = self.view(self.block(half, i, j), half, q)
        pltpu.make_async_copy(ref, ref, self.recv_sems.at[KEYS[(half, i, j, q)]]).wait()

    def start(self):
        for half in (0, 1):
            for d in (1, -1):
                self.copy(half, 0, 0, None, (d, 0), (half, -d, 0, None))
        for half in (0, 1):
            for d in (1, -1):
                self.copy(half, 0, 0, None, (0, d), (half, 0, -d, None))

    def first(self):
        for half in (0, 1):
            for d in (1, -1):
                q = 0 if d == 1 else 1
                self.wait(half, -d, 0, None)
                self.copy(half, -d, 0, q, (d, 0), (half, 2, 0, q))
                for e in (1, -1):
                    self.copy(half, -d, 0, None, (0, e), (half, -d, -e, None))

    def across(self, i):
        for half in (0, 1):
            for d in (1, -1):
                q = 0 if d == 1 else 1
                self.wait(half, i, -d, None)
                self.copy(half, i, -d, q, (0, d), (half, i, 2, q))

    def far(self):
        for half in (0, 1):
            for q in (0, 1):
                self.wait(half, 2, 0, q)
            for e in (1, -1):
                self.copy(half, 2, 0, None, (0, e), (half, 2, -e, None))

    def last(self, i):
        for half in (0, 1):
            for q in (0, 1):
                self.wait(half, i, 2, q)

    def drain(self):
        n = 0
        for whole in self.order():
            ref = self.view(0, 0, whole)
            pltpu.make_async_copy(ref, ref, self.send_sems.at[n]).wait()
            n += 1

    def order(self):
        sizes = [None] * 8
        for half in (0, 1):
            for d in (1, -1):
                sizes += [0 if d == 1 else 1, None, None]
        sizes += [0, 1] * 2
        sizes += [None] * 4
        sizes += [0, 1] * 2
        sizes += [0, 1] * 2
        sizes += [0, 1] * 2
        return sizes


PLANE = [(dx, dy) for dx in range(4) for dy in range(4) if (dx, dy) != (0, 0)]


def column_scale(tile, factor):
    parts = tile.astype(jnp.int32).astype(f32)
    return jnp.exp2(parts[:8]) * (parts[8:] * (factor / 32767.0))


def as_i16(value):
    return jnp.clip(jnp.round(value), -32767.0, 32767.0).astype(jnp.int32).astype(i16)


def iota(shape, axis):
    return lax.broadcasted_iota(jnp.int32, shape, axis)


def one_hot(test):
    return jnp.where(test, 1.0, 0.0).astype(bf16)


def dot(a, b, ca=1, cb=0):
    return lax.dot_general(a, b, (((ca,), (cb,)), ((), ())), preferred_element_type=f32)


def fill_outbox(env_ref, index_ref, count_ref, weight_ref, dest_ref, outbox):
    row = dest_ref[...]
    live = row >= 0
    dest = row >> 7
    owner = jnp.where(dest == iota((16, 256), 0), 1.0, 0.0)
    earlier = dot(owner.astype(bf16), one_hot(iota((256, 256), 0) < iota((256, 256), 1)))
    rank = jnp.sum(earlier * owner, axis=0, keepdims=True)
    place = jnp.where(live, dest.astype(f32) * 16.0 + rank, 999.0)
    move = one_hot(place == iota((256, 256), 0).astype(f32))
    env = env_ref[...]
    index = index_ref[...]
    envs = iota((512, 256), 0)
    picked = [dot(env, one_hot(index[j : j + 1] == envs)).astype(bf16) for j in range(4)]
    rest = jnp.where(iota((4, 256), 0) < count_ref[...], weight_ref[...], 0.0)
    meta = []
    for _ in range(3):
        part = rest.astype(bf16).astype(f32)
        rest = rest - part
        meta.append(part)
    within = jnp.where(live, (row & 127) + 1, 0).astype(f32)
    meta.append(jnp.where(iota((4, 256), 0) == 0, within, 0.0))
    meta.append(jnp.zeros((112, 256), f32))
    everything = jnp.concatenate(picked + [jnp.concatenate(meta, axis=0).astype(bf16)], axis=0)
    moved = dot(move, everything, 1, 1).astype(bf16)
    for d in range(16):
        for k in range(3):
            outbox[d, 16 * k : 16 * k + 16, :] = moved[16 * d : 16 * d + 16, 128 * k : 128 * k + 128]


def whole_kernel(env_ref, desc_ref, index_ref, count_ref, weight_ref, dest_ref, design_ref, out_ref,
                 points, outbox, inbox, feats, meta, lhs, buf, hp, lp, hrt, lrt,
                 psend, precv, osend, orecv, own_sem, fsend, frecv, frecv2, sends, recvs, middle, rsend, rrecv, tsend, trecv, zsend, zrecv, zsend2, zrecv2):
    x, y, z, c = where_am_i()
    r = x * 4 + y
    p = z * 2 + c
    lift = (7 * p + 16 - r) % 16
    drop = (7 * (p + r)) % 16
    source = (7 * r + 16 - p) % 16
    lifts, drops = lift != p, drop != r
    other = {"pts": z * 2 + 1 - c}
    along = {1: {"pts": ((z + 1) % 8) * 2 + c}, -1: {"pts": ((z + 7) % 8) * 2 + c}}
    beyond = {1: {"pts": ((z + 2) % 8) * 2 + c}, -1: {"pts": ((z + 6) % 8) * 2 + c}}
    barrier = pltpu.get_barrier_semaphore()
    for dx, dy in PLANE:
        pl.semaphore_signal(barrier, inc=1, device_id={"rows": plane_id(x, y, dx, dy)}, device_id_type=MESH)
    for d in (1, -1):
        pl.semaphore_signal(barrier, inc=1, device_id=along[d], device_id_type=MESH)

    for moves, targets in ((lifts, ({"pts": lift}, {"pts": drop})), (drops, ({"rows": drop}, {"rows": source}))):
        @pl.when(moves)
        def _():
            for target in targets:
                pl.semaphore_signal(barrier, inc=1, device_id=target, device_id_type=MESH)

    for target in (other, beyond[1], beyond[-1]):
        pl.semaphore_signal(barrier, inc=1, device_id=target, device_id_type=MESH)

    points[r, 0] = desc_ref[:32]
    points[r, 1] = desc_ref[32:]
    fill_outbox(env_ref, index_ref, count_ref, weight_ref, dest_ref, outbox)
    pl.semaphore_wait(barrier, 20 + jnp.where(lifts, 2, 0) + jnp.where(drops, 2, 0))

    def post(k, dx, dy):
        target = plane_id(x, y, dx, dy)
        return pltpu.make_async_remote_copy(
            src_ref=outbox.at[target], dst_ref=inbox.at[r], send_sem=osend.at[k], recv_sem=orecv.at[k],
            device_id={"rows": target}, device_id_type=MESH,
        )

    for k, (dx, dy) in enumerate(PLANE):
        post(k, dx, dy).start()
    own_copy = pltpu.make_async_copy(outbox.at[r], inbox.at[r], own_sem)
    own_copy.start()

    def points_view(block, half, q):
        return points.at[block, half] if q is None else points.at[block, half, pl.ds(16 * q, 16)]

    spread = TorusGather(x, y, points_view, psend, precv)
    spread.start()

    rows = r * 1024 + iota((128, 1024), 0)
    cols = p * 1024 + iota((128, 1024), 1)

    @pl.loop(0, 8)
    def _(m):
        out_ref[pl.ds(pl.multiple_of(m * 128, 128), 128), :] = jnp.where(rows + m * 128 == cols, damping, 0.0)

    spread.first()
    own_copy.wait()
    for k, (dx, dy) in enumerate(PLANE):
        ref = inbox.at[plane_id(x, y, -dx, -dy)]
        pltpu.make_async_copy(ref, ref, orecv.at[k]).wait()
    arrived = [jnp.concatenate([inbox[g, 16 * k : 16 * k + 16, :] for g in range(16)], axis=0) for k in range(3)]
    spots = arrived[2][:, 12:13].astype(f32)
    put = one_hot(spots == (iota((256, 128), 1) + 1).astype(f32))
    placed = dot(put, jnp.concatenate(arrived, axis=1), 0, 0)
    feats[p, 0] = placed[:, :128].astype(bf16)
    feats[p, 1] = placed[:, 128:256].astype(bf16)
    meta[...] = placed[:, 256:]

    def feat_copy(offset, pair, target, n, recv):
        ref = feats.at[((z + offset + 8) % 8) * 2 + c]
        if pair is not None:
            ref = ref.at[pair]
        return pltpu.make_async_remote_copy(
            src_ref=ref, dst_ref=ref, send_sem=fsend.at[n], recv_sem=recv, device_id=target, device_id_type=MESH
        )

    def feat_wait(owner, sem, pair=None):
        ref = feats.at[owner]
        if pair is not None:
            ref = ref.at[pair]
        pltpu.make_async_copy(ref, ref, sem).wait()

    for n, (target, recv) in enumerate((
        (along[1], frecv.at[0]), (along[-1], frecv.at[4]), (beyond[1], frecv.at[1]), (beyond[-1], frecv.at[5]),
        (other, frecv2.at[0]),
    )):
        feat_copy(0, None, target, n, recv).start()

    def feat_step(k):
        for d, base in ((1, 0), (-1, 4)):
            n = 4 * k + 1 + (0 if d == 1 else 2)
            feat_wait(((z - d * k + 8) % 8) * 2 + c, frecv.at[base + k - 1])
            if k < 3:
                pair = None if k == 1 else base // 4
                feat_copy(-d * k, pair, beyond[d], n, frecv.at[base + k + 1]).start()
            else:
                n = 12 if d == 1 else 13
            feat_copy(-d * k, None, other, n + 1, frecv2.at[(8 - d * k) % 8]).start()

    feat_step(1)
    spread.across(0)
    feat_step(2)
    spread.far()
    feat_step(3)
    spread.across(1)
    spread.across(-1)
    for d, base, pair in ((1, 0, 0), (-1, 4, 1)):
        feat_wait(((z + 4) % 8) * 2 + c, frecv.at[base + 3], pair)
    feat_copy(4, None, other, 15, frecv2.at[4]).start()
    for k in range(8):
        feat_wait(((z + k) % 8) * 2 + 1 - c, frecv2.at[k])
    spread.across(2)
    lane = iota((128, 128), 1)
    for k in range(8):
        for pair in (0, 1):
            a = feats[2 * k, pair].astype(f32)
            b = feats[2 * k + 1, pair].astype(f32)
            even = jnp.where(lane < 64, a, pltpu.roll(b, 64, 1))
            odd = jnp.where(lane < 64, pltpu.roll(a, 64, 1), b)
            lhs[pl.ds(pair * 256, 128), pl.ds(k * 128, 128)] = even.astype(bf16)
            lhs[pl.ds(pair * 256 + 128, 128), pl.ds(k * 128, 128)] = odd.astype(bf16)
    for i in (0, 1, -1, 2):
        spread.last(i)

    coeffs = meta[...]
    weights = [coeffs[:, j : j + 1] + coeffs[:, j + 4 : j + 5] + coeffs[:, j + 8 : j + 9] for j in range(4)]
    tops, bottoms = [], []
    for t in range(4):
        span = pl.ds(t * 256, 256)
        products = dot(lhs[...], points[:, :, :, span].reshape(1024, 256))
        scaled = products * (1.0 / 32.0)
        squared = scaled * scaled
        values = 0.25 * squared * squared
        line = jnp.zeros((128, 256), f32)
        for j in range(4):
            line = line + weights[j] * values[j * 128 : (j + 1) * 128]
        design_ref[:, span] = line
        largest = jnp.maximum(jnp.max(jnp.abs(line), axis=0, keepdims=True), 1e-30)
        exponent = jnp.floor(jnp.log2(largest)) - 14.0
        mantissa = jnp.minimum(jnp.ceil(largest * jnp.exp2(-exponent)), 32767.0)
        coded = line * (32767.0 / (mantissa * jnp.exp2(exponent)))
        for u in range(2):
            j = 2 * t + u
            part = as_i16(coded[:, 128 * u : 128 * u + 128])
            for half in (0, 1):
                buf[0, r, half, pl.ds(64 * j, 64), :] = part[64 * half : 64 * half + 64]
            tops.append(exponent[:, 128 * u : 128 * u + 128])
            bottoms.append(mantissa[:, 128 * u : 128 * u + 128])
    tile = as_i16(jnp.concatenate(tops + bottoms, axis=0))
    buf[0, r, 0, pl.ds(512, 16), :] = tile
    buf[0, r, 1, pl.ds(512, 16), :] = tile

    def panel_view(block, half, q):
        ref = buf.at[0, block, half]
        if q is None:
            return ref
        return ref.at[pl.ds(0, CUT)] if q == 0 else ref.at[pl.ds(CUT, HALF - CUT)]

    def rise(half):
        return pltpu.make_async_remote_copy(
            src_ref=buf.at[0, r, half], dst_ref=middle.at[half], send_sem=rsend.at[half], recv_sem=rrecv.at[half],
            device_id={"pts": lift}, device_id_type=MESH,
        )

    def turn(half):
        return pltpu.make_async_remote_copy(
            src_ref=middle.at[half], dst_ref=buf.at[1, p, half], send_sem=tsend.at[half], recv_sem=trecv.at[half],
            device_id={"rows": drop}, device_id_type=MESH,
        )

    for half in (0, 1):
        pl.when(lifts)(lambda: rise(half).start())
        pl.when(jnp.logical_not(lifts))(
            lambda: pltpu.make_async_copy(buf.at[0, r, half], middle.at[half], rrecv.at[half]).start()
        )

    gather = TorusGather(x, y, panel_view, sends, recvs)
    gather.start()

    def ring_copy(offset, half, target, send, recv):
        ref = buf.at[1, ((z + offset + 8) % 8) * 2 + c, half]
        return pltpu.make_async_remote_copy(
            src_ref=ref, dst_ref=ref, send_sem=send, recv_sem=recv, device_id=target, device_id_type=MESH
        )

    def half_wait(owner, half, sem):
        ref = buf.at[1, owner, half]
        pltpu.make_async_copy(ref, ref, sem).wait()

    def ring_step(k):
        for half in (0, 1):
            for d, side in ((1, 0), (-1, 1)):
                if k == 4 and half != side:
                    continue
                if k == 0:
                    if d == 1:
                        half_wait(p, half, trecv.at[half])
                else:
                    half_wait(((z - d * k + 8) % 8) * 2 + c, half, zrecv.at[side, k - 1, half])
                if k < 3 or (k == 3 and half == side):
                    ring_copy(-d * k, half, along[d], zsend.at[side, k, half], zrecv.at[side, k, half]).start()
                if k > 0 or d == 1:
                    o = (8 - d * k) % 8
                    ring_copy(o, half, other, zsend2.at[o, half], zrecv2.at[o, half]).start()

    def compute(o):
        zz = (z + o + 8) % 8
        for half in (0, 1):
            half_wait(2 * zz + 1 - c, half, zrecv2.at[(o + 8) % 8, half])
        for v in (0, 1):
            slot = 2 * zz + v
            scale = column_scale(buf[1, slot, 0, pl.ds(512, 16), :], 1.0)
            spot = pl.ds(v * 128, 128)
            for j in range(8):
                span = slice(128 * j, 128 * j + 128)
                hrt[span, spot], lrt[span, spot] = split_bf16(both_halves(1, slot, j, scale).T)
        first, second = (7 * r + 32 - 2 * zz) % 16, (7 * r + 31 - 2 * zz) % 16

        @pl.loop(0, 4)
        def _(t):
            span = pl.ds(pl.multiple_of(t * 256, 256), 256)
            high = hrt[...]
            left = jnp.concatenate([high, high, lrt[...]], axis=1)
            right_high = jnp.concatenate([hp[first, :, span], hp[second, :, span]], axis=0)
            right = jnp.concatenate([right_high, lp[first, :, span], lp[second, :, span], right_high], axis=0)
            out_ref[:, span] += dot(left, right)

    def both_halves(k, at, j, scale):
        parts = [buf[k, at, half, pl.ds(64 * j, 64), :] for half in (0, 1)]
        return jnp.concatenate(parts, axis=0).astype(jnp.int32).astype(f32) * scale[j : j + 1, :]

    def decode(steps):
        packed = sum((4 * dx + dy) << (4 * i) for i, (dx, dy) in enumerate(steps))

        @pl.loop(0, len(steps))
        def _(i):
            code = (jnp.int32(packed) >> (4 * i)) & 15
            b = plane_id(x, y, code // 4, code % 4)
            scale = column_scale(buf[0, b, 0, pl.ds(512, 16), :], 2.0 ** -11)
            for j in range(8):
                span = slice(128 * j, 128 * j + 128)
                hp[b, :, span], lp[b, :, span] = split_bf16(both_halves(0, b, j, scale))

    gather.first()
    for half in (0, 1):
        pltpu.make_async_copy(middle.at[half], middle.at[half], rrecv.at[half]).wait()
        pl.when(drops)(lambda: turn(half).start())
        pl.when(jnp.logical_not(drops))(
            lambda: pltpu.make_async_copy(middle.at[half], buf.at[1, p, half], trecv.at[half]).start()
        )
    gather.across(0)
    gather.far()
    decode([(0, 0), (1, 0), (3, 0), (0, 1), (0, 3)])
    gather.across(1)
    ring_step(0)
    gather.across(-1)
    gather.last(0)
    gather.across(2)
    decode([(1, 1), (1, 3), (3, 1), (3, 3), (2, 0), (0, 2)])
    ring_step(1)
    gather.last(1)
    gather.last(-1)
    gather.last(2)
    decode([(2, 1), (2, 3), (1, 2), (3, 2), (2, 2)])

    @pl.loop(0, 2)
    def _(i):
        compute(i)

    ring_step(2)

    @pl.loop(0, 2)
    def _(i):
        compute(3 * i - 1)

    ring_step(3)

    @pl.loop(0, 3)
    def _(i):
        compute(jnp.where(i == 0, -2, 9 - 6 * i))

    ring_step(4)
    compute(4)

    spread.drain()
    gather.drain()
    for k, (dx, dy) in enumerate(PLANE):
        post(k, dx, dy).wait_send()
    for n in range(16):
        feat_wait(0, fsend.at[n], 0 if n in (9, 11) else None)

    for half in (0, 1):
        pl.when(lifts)(lambda: rise(half).wait_send())
        pl.when(drops)(lambda: turn(half).wait_send())

    for half in (0, 1):
        for side in (0, 1):
            for k in range(4):
                if k < 3 or half == side:
                    half_wait(0, half, zsend.at[side, k, half])
        for o in range(8):
            half_wait(0, half, zsend2.at[o, half])


def on_device(env_desc, point_desc, pool_index, pool_count, pool_weight, row_dest):
    sem = pltpu.SemaphoreType.DMA
    return pl.pallas_call(
        whole_kernel,
        out_shape=(pltpu.VMEM((128, 1024), f32), pltpu.VMEM((1024, 1024), f32)),
        in_specs=[pl.BlockSpec(memory_space=VMEM)] * 6,
        out_specs=(pl.BlockSpec(memory_space=VMEM), pl.BlockSpec(memory_space=VMEM)),
        scratch_shapes=[
            VMEM((16, 2, 32, 1024), bf16),
            VMEM((16, 48, 128), bf16),
            VMEM((16, 48, 128), bf16),
            VMEM((16, 2, 128, 128), bf16),
            VMEM((128, 128), f32),
            VMEM((512, 1024), bf16),
            VMEM((2, 16, 2, HALF, 128), i16),
            VMEM((16, 128, 1024), bf16),
            VMEM((16, 128, 1024), bf16),
            VMEM((1024, 256), bf16),
            VMEM((1024, 256), bf16),
            sem((40,)), sem((40,)), sem((15,)), sem((15,)), sem(()), sem((16,)), sem((8,)), sem((8,)),
            sem((40,)), sem((40,)), VMEM((2, HALF, 128), i16),
            sem((2,)), sem((2,)), sem((2,)), sem((2,)), sem((2, 4, 2)), sem((2, 4, 2)), sem((8, 2)), sem((8, 2)),
        ],
        compiler_params=pltpu.CompilerParams(collective_id=1, has_side_effects=True, vmem_limit_bytes=56 << 20),
        name="whole",
    )(env_desc.T, point_desc.T, pool_index.T, pool_count.reshape(1, 256), pool_weight.T, row_dest.reshape(1, 256))


def solution(mesh):
    in_specs = (
        P("rows", "pts"),
        P("pts", "rows"),
        P("rows", None),
        P("rows"),
        P("rows", None),
        P("rows"),
    )
    out_specs = (P("rows", "pts"), P("rows", "pts"))
    return jax.shard_map(
        on_device, mesh=mesh, in_specs=in_specs, out_specs=out_specs, check_vma=False
    )
```
